32 devices in a mesh: tok: 4 (over z), row: 4 (over y, x), col: 2 (over core).
Axes of the slice: x: 2, y: 2, z: 4, core: 2. Of those that a mesh axis runs over, the one named last changes fastest.
Arguments:
- hidden_in: bfloat16 [4096, 2048], P(('tok', 'row', 'col')), may hold values from -6 to 6
- seg_ids: int32 [16, 256], P(('tok', 'row')), may hold values from 0 to 3, never falling along the last dimension, each value on 1 to 128 neighbouring positions
- expert_ids: int32 [4096, 8], P(('tok', 'row', 'col')), may hold values from 0 to 31, all different within a row; in each aligned block of 128 rows (0 to 127, 128 to 255, ...) at most 64 rows name the same one
- norm1_gain: float32 [2048], replicated, may hold values from 0.5 to 1.5
- query_gain: float32 [128], replicated, may hold values from 0.5 to 1.5
- key_gain: float32 [128], replicated, may hold values from 0.5 to 1.5
- w_query: bfloat16 [2048, 4096], P('row', 'col'), may hold values from -0.125 to 0.125
- w_keyval: bfloat16 [2048, 1024], P('row', 'col'), may hold values from -0.125 to 0.125
- w_output: bfloat16 [4096, 2048], P('col', 'row'), may hold values from -0.75 to 0.75
- norm2_gain: float32 [2048], replicated, may hold values from 0.5 to 1.5
- router: bfloat16 [2048, 32], replicated, may hold values from -0.0625 to 0.0625
- w_gate_up: bfloat16 [32, 2048, 1536], P(('tok', 'row', 'col')), may hold values from -0.125 to 0.125
- w_down: bfloat16 [32, 768, 2048], P(('tok', 'row', 'col')), may hold values from -0.875 to 0.875
- cotangent: bfloat16 [4096, 2048], P(('tok', 'row', 'col')), may hold values from -6 to 6
Outputs:
- layer_out: bfloat16 [4096, 2048], P(('tok', 'row', 'col'))
- input_grad: bfloat16 [4096, 2048], P(('tok', 'row', 'col'))
- w_query_grad: float32 [2048, 4096], P('row', 'col')
- w_keyval_grad: float32 [2048, 1024], P('row', 'col')
- w_output_grad: float32 [4096, 2048], P('col', 'row')
- router_grad: float32 [2048, 32], replicated
- gate_up_grad: float32 [32, 2048, 1536], P(('tok', 'row', 'col'))
- down_grad: float32 [32, 768, 2048], P(('tok', 'row', 'col'))
- norm1_grad: float32 [2048], replicated
- norm2_grad: float32 [2048], replicated
- query_gain_grad: float32 [128], replicated
- key_gain_grad: float32 [128], replicated
The draws below stay inside these ranges and needn't reach their ends.
Inputs may be any that keep to these rules, and one draw needn't show every extreme that they name: `seg_ids`: in each row the values never fall; each sequence has 1 to 128 tokens, and one has exactly 128. `expert_ids`: each row names 8 different experts; in the rows of one device (aligned blocks of 128 rows) no expert is named by more than 64 rows, a bound that some block reaches.
All inputs are finite; a program needn't handle non-finite values.
Results may differ from the reference program's by a relative error of at most 0.023.
Values may be sent and summed in bfloat16 or wider, within the bound.
No kernel may reach another device: no remote copies, remote signals or barrier semaphores. Data moves between devices by JAX's collectives and lax.ppermute only.
A program may use at most 256 MiB of HBM per device.

```python
import math
import jax
import jax.numpy as jnp
import numpy as np
from jax import lax

D = 2048
HQ = 32
KV = 4
HD = 128
FF = 768
TOPK = 8
TOK_DEV = 128
EXPERTS = 32
GROUP = 256
GROUPS = 16
TOKENS = 4096
SEQ_MAX = 128
SEQS = 4
CAP = 64


def level_of(key, dims, split, low, top_value):
    level = 1.0
    for dim, shards_of in split:
        draws = jax.random.uniform(jax.random.fold_in(jax.random.fold_in(key, 6), dim), (shards_of,), jnp.float32, low / len(split), top_value / len(split))
        level = level * jnp.repeat(jnp.exp(draws), dims[dim] // shards_of).reshape((-1,) + (1,) * (len(dims) - 1 - dim))
    return level


def split_up(amount, total, most, lean):
    weights = [(1 << 20) // math.isqrt(grade ** lean) + 1 for grade in range(2, amount + 1)]
    surplus, given = total - most - (amount - 1), [1] * (amount - 1)
    while surplus > 0:
        movable = [i for i in range(amount - 1) if given[i] < most]
        mass, remaining = sum([weights[i] for i in movable]), surplus
        for i in movable:
            extra = min(most - given[i], max(1, remaining * weights[i] // mass), surplus)
            given[i] = given[i] + extra
            surplus = surplus - extra
    return np.array([most] + given)


def ragged(stream_key, count, total, bound, skew):
    if count == 2:
        one = jax.random.randint(stream_key, (), max(1, total - bound), min(bound, total - 1) + 1)
        return jnp.stack([one, total - one])
    lengths = jnp.asarray(split_up(count, total, bound, skew), jnp.int32)
    pairs = (count - 1) // 2
    donor, receiver = lengths[1:1 + 2 * pairs:2], lengths[2:2 + 2 * pairs:2]
    margin = jnp.minimum(donor - 1, bound - receiver)
    passed = jax.random.randint(jax.random.fold_in(stream_key, 1), (pairs,), 0, 1 << 20) % (margin + 1)
    lengths = lengths.at[1:1 + 2 * pairs:2].set(donor - passed).at[2:2 + 2 * pairs:2].set(receiver + passed)
    return lengths[jax.random.permutation(jax.random.fold_in(stream_key, 2), count)]


def deal_out(own_key, own, number, rows, count, top, limit, skew):
    sequence = jax.random.permutation(own_key, count)
    packed, ordinary = portions_of(count, rows * top, limit, skew, True), portions_of(count, rows * top, limit, skew, False)
    places = jnp.arange(count)

    def named(lengths, rotation):
        used = int((lengths > 0).sum())
        fixed = max(1, used // 4)
        moved = fixed + (places - fixed + rotation * (used - fixed)) % max(1, count - fixed)
        return jnp.zeros((count,), jnp.int32).at[sequence[jnp.where(places < fixed, places, moved)]].set(jnp.asarray(lengths, jnp.int32))

    lengths = jnp.where(number % 4 == 0, named(packed, number // 4), named(ordinary, number - number // 4 - 1))
    mixed = jax.random.permutation(jax.random.fold_in(own, 3), count)
    source_of, receiver = mixed[0:count // 2 * 2:2], mixed[1:count // 2 * 2:2]
    room = jnp.minimum(lengths[source_of] - 1, limit - lengths[receiver]) // 2
    room = jnp.where((source_of == sequence[0]) | (receiver == sequence[0]) | (lengths[receiver] == 0), 0, jnp.maximum(room, 0))
    moved = jax.random.randint(jax.random.fold_in(own, 4), (count // 2,), 0, 1 << 20) % (room + 1)
    lengths = lengths.at[source_of].add(-moved).at[receiver].add(moved)
    members = jnp.searchsorted(jnp.cumsum(lengths), jnp.arange(rows * top), side="right").astype(jnp.int32)
    listing = members.reshape(top, rows).T
    listing = listing[jax.random.permutation(jax.random.fold_in(own, 1), rows)]
    rotation = jax.random.randint(jax.random.fold_in(own, 2), (rows, 1), 0, top)
    return jnp.take_along_axis(listing, (jnp.arange(top)[None, :] + rotation) % top, axis=1)


def portions_of(amount, total, limit, lean, full):
    loads = [(1 << 20) // math.isqrt(grade ** lean) + 1 for grade in range(1, amount + 1)]
    largest = limit if full else min(limit, max(-(-total // amount), total * loads[0] // sum(loads)))
    least = 1 if total - largest >= amount - 1 else 0
    holding, rest = [largest] + [least] * (amount - 1), total - largest - least * (amount - 1)
    while rest > 0:
        candidates = [i for i in range(1, amount) if holding[i] < largest] or [i for i in range(1, amount) if holding[i] < limit]
        mass, budget = sum([loads[i] for i in candidates]), rest
        for i in candidates:
            extra = min(limit - holding[i], max(1, budget * loads[i] // mass), rest)
            holding[i] = holding[i] + extra
            rest = rest - extra
    return np.array(holding)


def centred(key, dims, scale, limit, shards=(), kind=jnp.bfloat16):
    entries = scale * jax.random.normal(key, dims, jnp.float32)
    if shards:
        entries = entries * level_of(key, dims, shards, -0.22, 0.18)
    return jnp.clip(entries, -limit, limit).astype(kind)


def setup_inputs(seed: int = 0) -> dict:
    key_of = jax.random.split(jax.random.key(seed), 15)
    hidden_in = centred(key_of[0], (TOKENS, D), 1.0, 6.0, ((0, 32),))
    seg_ids = jax.vmap(lambda own: jnp.searchsorted(jnp.cumsum(ragged(own, SEQS, GROUP, SEQ_MAX, 2)), jnp.arange(GROUP), side="right"))(jax.random.split(key_of[1], GROUPS)).reshape((GROUPS, GROUP)).astype(jnp.int32)
    expert_ids_keys = jax.random.split(jax.random.fold_in(key_of[2], 1), TOKENS // TOK_DEV)
    expert_ids_turns = jax.random.permutation(jax.random.fold_in(key_of[2], 3), TOKENS // TOK_DEV)
    expert_ids = jax.vmap(lambda own, number: deal_out(jax.random.fold_in(key_of[2], 2), own, number, TOK_DEV, EXPERTS, TOPK, CAP, 1))(expert_ids_keys, expert_ids_turns).reshape((TOKENS, TOPK))
    norm1_gain = jnp.clip(1.0 + 0.1 * jax.random.normal(key_of[3], (D,), jnp.float32), 0.5, 1.5)
    query_gain = jnp.clip(1.0 + 0.1 * jax.random.normal(key_of[4], (HD,), jnp.float32), 0.5, 1.5)
    key_gain = jnp.clip(1.0 + 0.1 * jax.random.normal(key_of[5], (HD,), jnp.float32), 0.5, 1.5)
    w_query = centred(key_of[6], (D, HQ * HD), D ** -0.5, 0.125, ((0, 4), (1, 2)))
    w_keyval = centred(key_of[7], (D, 2 * KV * HD), D ** -0.5, 0.125, ((0, 4), (1, 2)))
    w_output = centred(key_of[8], (HQ * HD, D), (HQ * HD // 64) ** -0.5, 0.75, ((0, 2), (1, 4)))
    norm2_gain = jnp.clip(1.0 + 0.1 * jax.random.normal(key_of[9], (D,), jnp.float32), 0.5, 1.5)
    router = centred(key_of[10], (D, EXPERTS), (4 * D) ** -0.5, 0.0625)
    w_gate_up = centred(key_of[11], (EXPERTS, D, 2 * FF), D ** -0.5, 0.125, ((0, 32),))
    w_down = centred(key_of[12], (EXPERTS, FF, D), (FF // 16) ** -0.5, 0.875, ((0, 32),))
    cotangent = centred(key_of[13], (TOKENS, D), 1.0, 6.0, ((0, 32),))
    return dict(hidden_in=hidden_in, seg_ids=seg_ids, expert_ids=expert_ids, norm1_gain=norm1_gain, query_gain=query_gain, key_gain=key_gain, w_query=w_query, w_keyval=w_keyval, w_output=w_output, norm2_gain=norm2_gain, router=router, w_gate_up=w_gate_up, w_down=w_down, cotangent=cotangent)


EPSILON = 1e-06
ROPE_BASE = 1000000.0
PRECISE = lax.Precision.HIGHEST

def matmul(left, right):
    return jnp.dot(left, right, preferred_element_type=jnp.float32)

def product(form, left, right):
    return jnp.einsum(form, left.astype(jnp.float32), right.astype(jnp.float32), precision=PRECISE, preferred_element_type=jnp.float32)

def rms_scale(values, gain):
    return values * lax.rsqrt(lax.optimization_barrier(jnp.mean(values * values, axis=-1, keepdims=True)) + EPSILON) * gain

def positions_of(segment):
    length = segment.shape[0]
    positions_all = jnp.arange(length, dtype=jnp.int32)
    starts = jnp.concatenate([jnp.ones((1,), jnp.bool_), segment[1:] != segment[:-1]])
    first_index = lax.cummax(jnp.where(starts, positions_all, 0), axis=0)
    return positions_all - first_index

def rotary_tables(positions):
    half_width = HD // 2
    frequency = ROPE_BASE ** (-(jnp.arange(half_width, dtype=jnp.float32) * 2.0 / HD))
    angles = positions.astype(jnp.float32)[:, None] * frequency[None, :]
    return (jnp.cos(angles), jnp.sin(angles))

def norm_rotate(raw_part, gain_part, cosine_table, sine_table):
    row_count = raw_part.shape[0]
    head_rows = rms_scale(raw_part.reshape(row_count, -1, HD), gain_part)
    first_half = head_rows[..., :HD // 2]
    second_half = head_rows[..., HD // 2:]
    cosine_part = cosine_table[:, None, :]
    sine_part = sine_table[:, None, :]
    turned = jnp.concatenate([first_half * cosine_part - second_half * sine_part, second_half * cosine_part + first_half * sine_part], axis=-1)
    return turned.reshape(row_count, -1)

def window_setup(key_rows, value_rows, segment, block_rows):
    key_pad = jnp.concatenate([jnp.zeros((block_rows, key_rows.shape[1]), key_rows.dtype), key_rows], axis=0)
    value_pad = jnp.concatenate([jnp.zeros((block_rows, value_rows.shape[1]), value_rows.dtype), value_rows], axis=0)
    seg_pad = jnp.concatenate([jnp.full((block_rows,), -1, jnp.int32), segment.astype(jnp.int32)])
    return (key_pad, value_pad, seg_pad)

def block_view(queries, key_pad, value_pad, segment, seg_pad, row_start, block_rows, head_map):
    head_count = queries.shape[1] // HD
    query_blk = lax.dynamic_slice_in_dim(queries, row_start, block_rows, 0).reshape(block_rows, head_count, HD)
    key_blk = lax.dynamic_slice_in_dim(key_pad, row_start, 2 * block_rows, 0).reshape(2 * block_rows, -1, HD)[:, head_map, :]
    value_blk = lax.dynamic_slice_in_dim(value_pad, row_start, 2 * block_rows, 0).reshape(2 * block_rows, -1, HD)[:, head_map, :]
    seg_query = lax.dynamic_slice_in_dim(segment, row_start, block_rows, 0)
    seg_key = lax.dynamic_slice_in_dim(seg_pad, row_start, 2 * block_rows, 0)
    query_idx = row_start + jnp.arange(block_rows, dtype=jnp.int32)
    key_idx = row_start - block_rows + jnp.arange(2 * block_rows, dtype=jnp.int32)
    allowed = (seg_query[:, None] == seg_key[None, :]) & (key_idx[None, :] <= query_idx[:, None])
    return (query_blk, key_blk, value_blk, allowed)

def attend(queries, key_rows, value_rows, segment, group_size, block_rows):
    row_count = queries.shape[0]
    head_count = queries.shape[1] // HD
    head_map = np.arange(head_count) // group_size
    score_scale = 1.0 / math.sqrt(HD)
    key_pad, value_pad, seg_pad = window_setup(key_rows, value_rows, segment, block_rows)

    def one_block(block_index):
        row_start = block_index * block_rows
        query_blk, key_blk, value_blk, allowed = block_view(queries, key_pad, value_pad, segment, seg_pad, row_start, block_rows, head_map)
        scores = product('qhd,khd->hqk', query_blk, key_blk) * score_scale
        raised = jnp.where(allowed[None], jnp.exp(scores), 0.0)
        denominator = lax.optimization_barrier(jnp.sum(raised, axis=-1, keepdims=True))
        attention = (raised / denominator).astype(jnp.bfloat16)
        mixed_blk = product('hqk,khd->qhd', attention, value_blk)
        return (mixed_blk.astype(jnp.bfloat16).reshape(block_rows, head_count * HD), jnp.log(denominator[..., 0]))
    mixed_out, log_total = lax.map(one_block, jnp.arange(row_count // block_rows, dtype=jnp.int32))
    return (mixed_out.reshape(row_count, head_count * HD), log_total)

def attend_back(queries, key_rows, value_rows, segment, mixed_out, mixed_grad, log_total, group_size, block_rows):
    row_count = queries.shape[0]
    head_count = queries.shape[1] // HD
    kv_count = key_rows.shape[1] // HD
    head_map = np.arange(head_count) // group_size
    score_scale = 1.0 / math.sqrt(HD)
    key_pad, value_pad, seg_pad = window_setup(key_rows, value_rows, segment, block_rows)

    def fold_heads(per_head):
        return per_head.reshape(2 * block_rows, kv_count, head_count // kv_count, HD).sum(axis=2).reshape(2 * block_rows, kv_count * HD)

    def one_block(state_now, inputs):
        key_acc, value_acc = state_now
        block_index, log_block = inputs
        row_start = block_index * block_rows
        query_blk, key_blk, value_blk, allowed = block_view(queries, key_pad, value_pad, segment, seg_pad, row_start, block_rows, head_map)
        scores = product('qhd,khd->hqk', query_blk, key_blk) * score_scale
        weights = jnp.where(allowed[None], jnp.exp(scores - log_block[:, :, None]), 0.0)
        attention = weights.astype(jnp.bfloat16)
        grad_blk = lax.dynamic_slice_in_dim(mixed_grad, row_start, block_rows, 0).reshape(block_rows, head_count, HD)
        out_blk = lax.dynamic_slice_in_dim(mixed_out, row_start, block_rows, 0).reshape(block_rows, head_count, HD)
        value_head = product('hqk,qhd->khd', attention, grad_blk)
        weight_grad = product('qhd,khd->hqk', grad_blk, value_blk)
        delta = lax.optimization_barrier(jnp.sum(grad_blk.astype(jnp.float32) * out_blk.astype(jnp.float32), axis=-1)).T
        score_grad = (weights * (weight_grad - delta[:, :, None])).astype(jnp.bfloat16)
        query_grad = product('hqk,khd->qhd', score_grad, key_blk) * score_scale
        key_head = product('hqk,qhd->khd', score_grad, query_blk) * score_scale
        key_acc = lax.dynamic_update_slice_in_dim(key_acc, lax.dynamic_slice_in_dim(key_acc, row_start, 2 * block_rows, 0) + fold_heads(key_head), row_start, 0)
        value_acc = lax.dynamic_update_slice_in_dim(value_acc, lax.dynamic_slice_in_dim(value_acc, row_start, 2 * block_rows, 0) + fold_heads(value_head), row_start, 0)
        return ((key_acc, value_acc), query_grad.reshape(block_rows, head_count * HD))
    zero_acc = jnp.zeros((row_count + block_rows, kv_count * HD), jnp.float32)
    block_ids = jnp.arange(row_count // block_rows, dtype=jnp.int32)
    (key_acc, value_acc), query_back = lax.scan(one_block, (zero_acc, zero_acc), (block_ids, log_total))
    return (query_back.reshape(row_count, head_count * HD), key_acc[block_rows:], value_acc[block_rows:])

def reference(hidden_in, seg_ids, expert_ids, norm1_gain, query_gain, key_gain, w_query, w_keyval, w_output, norm2_gain, router, w_gate_up, w_down, cotangent):
    group_size = HQ // KV
    key_cols = KV * HD
    grouped = hidden_in.reshape(GROUPS, GROUP, D)

    def attn_forward(segment, tokens):
        floats = tokens.astype(jnp.float32)
        normed = rms_scale(floats, norm1_gain).astype(jnp.bfloat16)
        query_raw = matmul(normed, w_query)
        keyval = matmul(normed, w_keyval).astype(jnp.bfloat16)
        cosine_table, sine_table = rotary_tables(positions_of(segment))
        queries = norm_rotate(query_raw, query_gain, cosine_table, sine_table).astype(jnp.bfloat16)
        key_raw = keyval[:, :key_cols].astype(jnp.float32)
        key_rows = norm_rotate(key_raw, key_gain, cosine_table, sine_table).astype(jnp.bfloat16)
        value_rows = keyval[:, key_cols:]
        mixed_out, log_total = attend(queries, key_rows, value_rows, segment, group_size, SEQ_MAX)
        return (floats, normed, query_raw, key_raw, value_rows, cosine_table, sine_table, queries, key_rows, mixed_out, log_total)

    def residual_one(inputs):
        parts = attn_forward(inputs[0], inputs[1])
        return parts[0] + matmul(parts[9], w_output)
    after_attn = lax.map(residual_one, (seg_ids, grouped)).reshape(TOKENS, D)
    normed2 = rms_scale(after_attn, norm2_gain).astype(jnp.bfloat16)
    logits = matmul(normed2, router)
    picked = jnp.take_along_axis(logits, expert_ids, axis=1)
    raised = jnp.exp(picked)
    gate_weights = raised / lax.optimization_barrier(jnp.sum(raised, axis=1, keepdims=True))
    device_total = TOKENS // TOK_DEV
    pair_count = TOK_DEV * TOPK
    pair_expert = expert_ids.reshape(device_total, pair_count)
    onehot = (pair_expert[:, :, None] == jnp.arange(EXPERTS, dtype=jnp.int32)[None, None, :]).astype(jnp.int32)
    earlier = lax.optimization_barrier(jnp.sum((jnp.cumsum(onehot, axis=1) - onehot) * onehot, axis=2))
    slot_index = pair_expert * CAP + earlier
    device_idx = jnp.arange(device_total, dtype=jnp.int32)[:, None]
    pair_global = device_idx * pair_count + jnp.arange(pair_count, dtype=jnp.int32)[None, :]
    slot_pair = jnp.zeros((device_total, EXPERTS * CAP), jnp.int32).at[device_idx, slot_index].set(pair_global)
    slot_live = jnp.zeros((device_total, EXPERTS * CAP), jnp.float32).at[device_idx, slot_index].set(1.0)
    slot_pair = slot_pair.reshape(device_total, EXPERTS, CAP).transpose(1, 0, 2).reshape(EXPERTS, device_total * CAP)
    slot_live = slot_live.reshape(device_total, EXPERTS, CAP).transpose(1, 0, 2).reshape(EXPERTS, device_total * CAP)
    gate_flat = gate_weights.reshape(-1)
    grad_out = cotangent.astype(jnp.float32)

    def expert_step(state_now, inputs):
        mixture, gate_grad, rows_grad = state_now
        pair_ids, live_rows, weight_gu, weight_down = inputs
        token_ids = pair_ids // TOPK
        rows_in = jnp.where(live_rows[:, None] > 0, normed2[token_ids], 0.0).astype(jnp.bfloat16)
        joined = matmul(rows_in, weight_gu)
        gate_part = joined[:, :FF]
        up_part = joined[:, FF:]
        sigmoid_gate = jax.nn.sigmoid(gate_part)
        hidden = (gate_part * sigmoid_gate * up_part).astype(jnp.bfloat16)
        result = matmul(hidden, weight_down).astype(jnp.bfloat16).astype(jnp.float32)
        weight_row = gate_flat[pair_ids] * live_rows
        grad_rows = grad_out[token_ids]
        mixture = mixture.at[token_ids].add(weight_row[:, None] * result)
        gate_grad = gate_grad.at[pair_ids].add(live_rows * lax.optimization_barrier(jnp.sum(grad_rows * result, axis=1)))
        result_grad = (weight_row[:, None] * grad_rows).astype(jnp.bfloat16)
        hidden_grad = matmul(result_grad, weight_down.T)
        down_part = matmul(hidden.T, result_grad)
        gate_back = hidden_grad * up_part * sigmoid_gate * (1.0 + gate_part * (1.0 - sigmoid_gate))
        up_back = hidden_grad * gate_part * sigmoid_gate
        joined_grad = jnp.concatenate([gate_back, up_back], axis=1).astype(jnp.bfloat16)
        gu_part = matmul(rows_in.T, joined_grad)
        back_rows = matmul(joined_grad, weight_gu.T).astype(jnp.bfloat16).astype(jnp.float32)
        rows_grad = rows_grad.at[token_ids].add(back_rows * live_rows[:, None])
        return ((mixture, gate_grad, rows_grad), (gu_part, down_part))
    start_state = (jnp.zeros((TOKENS, D), jnp.float32), jnp.zeros((TOKENS * TOPK,), jnp.float32), jnp.zeros((TOKENS, D), jnp.float32))
    (mixture, gate_grad, rows_grad), (gate_up_grad, down_grad) = lax.scan(expert_step, start_state, (slot_pair, slot_live, w_gate_up, w_down))
    layer_out = (after_attn + mixture).astype(jnp.bfloat16)
    gate_grad = gate_grad.reshape(TOKENS, TOPK)
    pick_grad = gate_weights * (gate_grad - lax.optimization_barrier(jnp.sum(gate_weights * gate_grad, axis=1, keepdims=True)))
    chosen = expert_ids[:, :, None] == jnp.arange(EXPERTS, dtype=jnp.int32)[None, None, :]
    logit_grad = lax.optimization_barrier(jnp.sum(jnp.where(chosen, pick_grad[:, :, None], 0.0), axis=1)).astype(jnp.bfloat16)
    router_grad = matmul(normed2.T, logit_grad)
    normed2_grad = rows_grad + matmul(logit_grad, router.T)
    _, norm2_back = jax.vjp(rms_scale, after_attn, norm2_gain)
    resid_grad, norm2_grad = norm2_back(normed2_grad)
    resid_grad = resid_grad + grad_out

    def attn_backward(state_now, inputs):
        query_acc, keyval_acc, output_acc, gain1_acc, qgain_acc, kgain_acc = state_now
        segment, tokens, resid_rows = inputs
        floats, normed, query_raw, key_raw, value_rows, cosine_table, sine_table, queries, key_rows, mixed_out, log_total = attn_forward(segment, tokens)
        out_grad = resid_rows.astype(jnp.bfloat16)
        output_acc = output_acc + matmul(mixed_out.T, out_grad)
        mixed_grad = matmul(out_grad, w_output.T).astype(jnp.bfloat16)
        query_back, key_back, value_back = attend_back(queries, key_rows, value_rows, segment, mixed_out, mixed_grad, log_total, group_size, SEQ_MAX)
        _, query_fn = jax.vjp(lambda raw_part, gain_part: norm_rotate(raw_part, gain_part, cosine_table, sine_table), query_raw, query_gain)
        query_raw_grad, qgain_part = query_fn(query_back)
        _, key_fn = jax.vjp(lambda raw_part, gain_part: norm_rotate(raw_part, gain_part, cosine_table, sine_table), key_raw, key_gain)
        key_raw_grad, kgain_part = key_fn(key_back)
        query_send = query_raw_grad.astype(jnp.bfloat16)
        keyval_send = jnp.concatenate([key_raw_grad, value_back], axis=1).astype(jnp.bfloat16)
        query_acc = query_acc + matmul(normed.T, query_send)
        keyval_acc = keyval_acc + matmul(normed.T, keyval_send)
        normed_grad = matmul(query_send, w_query.T) + matmul(keyval_send, w_keyval.T)
        _, norm1_back = jax.vjp(rms_scale, floats, norm1_gain)
        floats_grad, gain1_part = norm1_back(normed_grad)
        input_rows = (resid_rows + floats_grad).astype(jnp.bfloat16)
        new_state = (query_acc, keyval_acc, output_acc, gain1_acc + gain1_part, qgain_acc + qgain_part, kgain_acc + kgain_part)
        return (new_state, input_rows)
    start_state = (jnp.zeros((D, HQ * HD), jnp.float32), jnp.zeros((D, 2 * KV * HD), jnp.float32), jnp.zeros((HQ * HD, D), jnp.float32), jnp.zeros((D,), jnp.float32), jnp.zeros((HD,), jnp.float32), jnp.zeros((HD,), jnp.float32))
    final_state, input_grad = lax.scan(attn_backward, start_state, (seg_ids, grouped, resid_grad.reshape(GROUPS, GROUP, D)))
    w_query_grad, w_keyval_grad, w_output_grad, norm1_grad, query_gain_grad, key_gain_grad = final_state
    return (layer_out, input_grad.reshape(TOKENS, D), w_query_grad, w_keyval_grad, w_output_grad, router_grad, gate_up_grad, down_grad, norm1_grad, norm2_grad, query_gain_grad, key_gain_grad)
```

```python
import functools
import math

import jax
import jax.numpy as jnp
from jax import lax
from jax.experimental import pallas as pl
from jax.experimental.pallas import tpu as pltpu
from jax.sharding import PartitionSpec as P

D = 2048
HQ = 32
KV = 4
HD = 128
FF = 768
TOPK = 8
EPSILON = 1e-06
ROPE_BASE = 1000000.0
BF = jnp.bfloat16
F32 = jnp.float32
ALL = ("tok", "row", "col")


def matmul(left, right):
    return jnp.dot(left, right, preferred_element_type=F32)


def contract(left, right, dims):
    return lax.dot_general(left, right, (dims, ((), ())), preferred_element_type=F32)


def rms_scale(values, gain):
    return values * lax.rsqrt(jnp.mean(values * values, axis=-1, keepdims=True) + EPSILON) * gain


def total(*parts):
    acc = parts[0].astype(F32)
    for part in parts[1:]:
        acc = acc + part.astype(F32)
    return acc


def flip(values, axis, mask, size):
    return lax.ppermute(values, axis, [(i, i ^ mask) for i in range(size)])


def turn(rows, cos_ref, sin_ref):
    return rows * cos_ref[0] + pltpu.roll(rows, HD // 2, 1) * sin_ref[0]


def turn_back(rows, cos_ref, sin_ref):
    return rows * cos_ref[0] + pltpu.roll(rows * sin_ref[0], HD // 2, 1)


def inverse_rms(rows):
    return lax.rsqrt(jnp.mean(rows * rows, axis=-1, keepdims=True) + EPSILON)


def head_of(ref, head):
    part = ref[:, 0, :, head * HD : (head + 1) * HD]
    return part.reshape(part.shape[0] * part.shape[1], HD)


def put_head(ref, head, rows):
    shape = ref.shape
    ref[:, 0, :, head * HD : (head + 1) * HD] = rows.reshape(shape[0], shape[2], HD).astype(
        ref.dtype
    )


def softmax_of(query_rows, key_rows, mask_ref):
    scores = contract(query_rows, key_rows, ((1,), (1,))) * (1.0 / math.sqrt(HD))
    raised = jnp.where(mask_ref[0] > 0.0, jnp.exp(scores), 0.0)
    return raised / jnp.sum(raised, axis=-1, keepdims=True)


def attend_kernel(heads, q_ref, kv_ref, cos_ref, sin_ref, mask_ref, qg_ref, kg_ref, out_ref):
    key_raw = head_of(kv_ref, 0).astype(F32)
    value_rows = head_of(kv_ref, 1)
    key_rows = turn(key_raw * inverse_rms(key_raw) * kg_ref[...], cos_ref, sin_ref).astype(BF)
    for head in range(heads):
        raw = head_of(q_ref, head)
        query_rows = turn(raw * inverse_rms(raw) * qg_ref[...], cos_ref, sin_ref).astype(BF)
        attention = softmax_of(query_rows, key_rows, mask_ref).astype(BF)
        put_head(out_ref, head, contract(attention, value_rows, ((1,), (0,))))


def rms_back(raw, inverse, gain, grad):
    scaled = grad * gain
    inner = jnp.sum(scaled * raw, axis=-1, keepdims=True) * (1.0 / HD)
    raw_grad = inverse * scaled - raw * (inverse * inverse * inverse * inner)
    return raw_grad, jnp.sum(grad * raw * inverse, axis=0, keepdims=True)


def attend_back_kernel(
    heads,
    q_ref,
    kv_ref,
    cos_ref,
    sin_ref,
    mask_ref,
    qg_ref,
    kg_ref,
    mixed_ref,
    grad_ref,
    qsend_ref,
    kvsend_ref,
    qgain_ref,
    kgain_ref,
):
    scale = 1.0 / math.sqrt(HD)
    key_raw = head_of(kv_ref, 0).astype(F32)
    value_rows = head_of(kv_ref, 1)
    key_inverse = inverse_rms(key_raw)
    key_rows = turn(key_raw * key_inverse * kg_ref[...], cos_ref, sin_ref).astype(BF)
    key_back = jnp.zeros(key_raw.shape, F32)
    value_back = jnp.zeros(key_raw.shape, F32)
    gain_sum = jnp.zeros((1, HD), F32)
    for head in range(heads):
        raw = head_of(q_ref, head)
        inverse = inverse_rms(raw)
        query_rows = turn(raw * inverse * qg_ref[...], cos_ref, sin_ref).astype(BF)
        weights = softmax_of(query_rows, key_rows, mask_ref)
        grad = head_of(grad_ref, head)
        mixed = head_of(mixed_ref, head)
        value_back = value_back + contract(weights.astype(BF), grad, ((0,), (0,)))
        weight_grad = contract(grad, value_rows, ((1,), (1,)))
        delta = jnp.sum(grad.astype(F32) * mixed.astype(F32), axis=-1, keepdims=True)
        score_grad = (weights * (weight_grad - delta)).astype(BF)
        query_back = contract(score_grad, key_rows, ((1,), (0,))) * scale
        key_back = key_back + contract(score_grad, query_rows, ((0,), (0,))) * scale
        raw_grad, gain_part = rms_back(
            raw, inverse, qg_ref[...], turn_back(query_back, cos_ref, sin_ref)
        )
        gain_sum = gain_sum + gain_part
        put_head(qsend_ref, head, raw_grad)
    key_grad, kgain_part = rms_back(
        key_raw, key_inverse, kg_ref[...], turn_back(key_back, cos_ref, sin_ref)
    )
    put_head(kvsend_ref, 0, key_grad)
    put_head(kvsend_ref, 1, value_back)

    @pl.when(pl.program_id(0) == 0)
    def _():
        qgain_ref[...] = jnp.zeros_like(qgain_ref)
        kgain_ref[...] = jnp.zeros_like(kgain_ref)

    qgain_ref[...] += gain_sum
    kgain_ref[...] += kgain_part


def group_spec(shape):
    return pl.BlockSpec((shape[0], 1) + shape[2:], lambda g: (0, g, 0, 0))


def table_spec(shape):
    return pl.BlockSpec((1,) + shape[1:], lambda g: (g, 0, 0))


def whole_spec(shape):
    return pl.BlockSpec(shape, lambda g: (0,) * len(shape))


def attention_specs(query_raw, keyval, cosine, sine, mask):
    return [
        group_spec(query_raw.shape),
        group_spec(keyval.shape),
        table_spec(cosine.shape),
        table_spec(sine.shape),
        table_spec(mask.shape),
        whole_spec((1, HD)),
        whole_spec((1, HD)),
    ]


def attend(heads, query_raw, keyval, cosine, sine, mask, qg, kg):
    return pl.pallas_call(
        functools.partial(attend_kernel, heads),
        grid=(query_raw.shape[1],),
        in_specs=attention_specs(query_raw, keyval, cosine, sine, mask),
        out_specs=group_spec(query_raw.shape),
        out_shape=jax.ShapeDtypeStruct(query_raw.shape, BF),
        compiler_params=pltpu.CompilerParams(vmem_limit_bytes=56 << 20),
        name="attend",
    )(query_raw, keyval, cosine, sine, mask, qg, kg)


def attend_back(heads, query_raw, keyval, cosine, sine, mask, qg, kg, mixed, grad):
    return pl.pallas_call(
        functools.partial(attend_back_kernel, heads),
        grid=(query_raw.shape[1],),
        in_specs=attention_specs(query_raw, keyval, cosine, sine, mask)
        + [group_spec(mixed.shape), group_spec(grad.shape)],
        out_specs=[
            group_spec(query_raw.shape),
            group_spec(keyval.shape),
            whole_spec((1, HD)),
            whole_spec((1, HD)),
        ],
        out_shape=[
            jax.ShapeDtypeStruct(query_raw.shape, BF),
            jax.ShapeDtypeStruct(keyval.shape, BF),
            jax.ShapeDtypeStruct((1, HD), F32),
            jax.ShapeDtypeStruct((1, HD), F32),
        ],
        compiler_params=pltpu.CompilerParams(vmem_limit_bytes=56 << 20),
        name="attend_back",
    )(query_raw, keyval, cosine, sine, mask, qg, kg, mixed, grad)


def pick_kernel(blocks, experts, capacity, scaled, *refs):
    pieces = refs[:blocks]
    rank_ref = refs[blocks]
    weight_ref = refs[blocks + 1] if scaled else None
    outs = refs[blocks + 1 + scaled :]
    rows = pieces[0].shape[0]
    slots = lax.broadcasted_iota(jnp.int32, (capacity, rows), 0).astype(F32)
    for block in range(blocks):
        hit = [
            (slots == rank_ref[block, e : e + 1, :]).astype(F32) for e in range(experts)
        ]
        select = jnp.concatenate(hit, axis=0).astype(BF)
        if scaled:
            level = jnp.concatenate(
                [
                    jnp.sum(hit[e] * weight_ref[block, e : e + 1, :], axis=1, keepdims=True)
                    for e in range(experts)
                ],
                axis=0,
            )
        chunk = 512

        def body(step, carry, block=block, select=select):
            cols = pl.ds(pl.multiple_of(step * chunk, chunk), chunk)
            picked = matmul(select, pieces[block][:, cols])
            if scaled:
                picked = picked * level
            picked = picked.astype(BF)
            for e in range(experts):
                outs[e][block * capacity : (block + 1) * capacity, cols] = picked[
                    e * capacity : (e + 1) * capacity
                ]
            return carry

        lax.fori_loop(0, pieces[block].shape[1] // chunk, body, 0)


def pick(pieces, rank, capacity, weight=None):
    blocks, experts = rank.shape[0], rank.shape[1]
    operands = list(pieces) + [rank] + ([] if weight is None else [weight])
    shape = jax.ShapeDtypeStruct((blocks * capacity, pieces[0].shape[1]), BF)
    return pl.pallas_call(
        functools.partial(pick_kernel, blocks, experts, capacity, int(weight is not None)),
        in_specs=[pl.BlockSpec(memory_space=pltpu.VMEM)] * len(operands),
        out_specs=[pl.BlockSpec(memory_space=pltpu.VMEM)] * experts,
        out_shape=[shape] * experts,
        compiler_params=pltpu.CompilerParams(vmem_limit_bytes=48 << 20),
        name="pick",
    )(*operands)


def spread_kernel(blocks, experts, capacity, scaled, *refs):
    rows_refs = refs[:experts]
    rank_ref = refs[experts]
    weight_ref = refs[experts + 1] if scaled else None
    outs = refs[experts + 1 + scaled :]
    tokens = outs[0].shape[0]
    slots = lax.broadcasted_iota(jnp.int32, (tokens, capacity), 1).astype(F32)
    for block in range(blocks):
        hit = [
            (slots == rank_ref[block, :, e : e + 1]).astype(F32).astype(BF)
            for e in range(experts)
        ]
        chunk = 512

        def body(step, carry, block=block, hit=hit):
            cols = pl.ds(pl.multiple_of(step * chunk, chunk), chunk)
            acc = None
            for e in range(experts):
                part = matmul(
                    hit[e], rows_refs[e][block * capacity : (block + 1) * capacity, cols]
                )
                if scaled:
                    part = part * weight_ref[block, :, e : e + 1]
                acc = part if acc is None else acc + part
            outs[block][:, cols] = acc.astype(BF)
            return carry

        lax.fori_loop(0, outs[block].shape[1] // chunk, body, 0)


def spread(rows, rank, capacity, weight=None):
    blocks, tokens, experts = rank.shape
    operands = list(rows) + [rank] + ([] if weight is None else [weight])
    shape = jax.ShapeDtypeStruct((tokens, rows[0].shape[1]), BF)
    return pl.pallas_call(
        functools.partial(spread_kernel, blocks, experts, capacity, int(weight is not None)),
        in_specs=[pl.BlockSpec(memory_space=pltpu.VMEM)] * len(operands),
        out_specs=[pl.BlockSpec(memory_space=pltpu.VMEM)] * blocks,
        out_shape=[shape] * blocks,
        compiler_params=pltpu.CompilerParams(vmem_limit_bytes=48 << 20),
        name="spread",
    )(*operands)


def build(sizes):
    nt, nr, nc = sizes["tok"], sizes["row"], sizes["col"]
    assert nt == 4 and nr == 4

    def tok(values, mask):
        return flip(values, "tok", mask, nt)

    def row(values, mask):
        return flip(values, "row", mask, nr)

    def col(values, mask):
        return flip(values, "col", mask, nc)

    def gather16(own):
        first, second = tok(own, 1), tok(own, 2)
        base = [own, first, second, tok(second, 1)]
        ones = [row(part, 1) for part in base]
        twos = [row(part, 2) for part in base]
        threes = [row(twos[0], 1), row(ones[1], 2), row(twos[2], 1), row(ones[3], 2)]
        return [part for z in range(4) for part in (base[z], ones[z], twos[z], threes[z])]

    def reduce16(parts):
        p = [list(parts[4 * z : 4 * z + 4]) for z in range(4)]

        def narrow(*values):
            return total(*values).astype(BF)

        p[3][1] = narrow(p[3][1], row(p[3][3], 2))
        p[2][2] = narrow(p[2][2], row(p[2][3], 1))
        p[1][1] = narrow(p[1][1], row(p[1][3], 2))
        p[0][2] = narrow(p[0][2], row(p[0][3], 1))
        for z in (3, 2, 1, 0):
            received = (row(p[z][1], 1), row(p[z][2], 2))
            p[z][0] = total(p[z][0], *received) if z == 0 else narrow(p[z][0], *received)
        p[2][0] = narrow(p[2][0], tok(p[3][0], 1))
        return total(p[0][0], tok(p[1][0], 1), tok(p[2][0], 2))

    def plane_gather(own):
        rows = lax.all_to_all(jnp.broadcast_to(own[None], (nr,) + own.shape), "row", 0, 0)
        return [rows] + [col(rows, m) for m in range(1, nc)]

    def plane_scatter(parts):
        mine = total(parts[0], *[col(parts[m], m) for m in range(1, nc)]).astype(BF)
        return jnp.sum(lax.all_to_all(mine, "row", 0, 0).astype(F32), axis=0)

    def tok_scatter(values, place):
        rel = [
            lax.dynamic_index_in_dim(values, place ^ m, 0, keepdims=False).astype(BF)
            for m in range(4)
        ]
        from_three = tok(rel[3], 1)
        from_one = tok(rel[1], 1)
        second = total(rel[2], from_three).astype(BF)
        return total(rel[0], from_one, tok(second, 2)).astype(BF)

    def tok_gather(own, place):
        second = tok(own, 2)
        rel = [own, tok(own, 1), second, tok(second, 1)]
        out = jnp.zeros((nt,) + own.shape, F32)
        for m in range(4):
            out = lax.dynamic_update_index_in_dim(out, rel[m].astype(F32), place ^ m, 0)
        return out

    def sum_small(values):
        devices = nt * nr * nc
        length = values.shape[0]
        width = -(-length // (devices * 128)) * 128
        padded = jnp.concatenate([values, jnp.zeros((devices * width - length,), F32)])
        mine = jnp.sum(lax.all_to_all(padded.reshape(devices, width), ALL, 0, 0), axis=0)
        back = lax.all_to_all(jnp.broadcast_to(mine[None], (devices, width)), ALL, 0, 0)
        return back.reshape(-1)[:length]

    def per_device(
        hidden_in,
        seg_ids,
        expert_ids,
        norm1_gain,
        query_gain,
        key_gain,
        w_query,
        w_keyval,
        w_output,
        norm2_gain,
        router,
        w_gate_up,
        w_down,
        cotangent,
    ):
        tok_i, row_i, col_i = (lax.axis_index(name) for name in ALL)
        experts = router.shape[1]
        tokens = hidden_in.shape[0]
        capacity = max(2, 2 * tokens * TOPK // experts)
        heads = HQ // (nr * nc)
        group_size = HQ // KV
        head_cols = heads * HD
        group = seg_ids.shape[1]
        key_cols = KV * HD

        chosen = jnp.any(
            expert_ids[:, :, None] == jnp.arange(experts, dtype=jnp.int32)[None, None, :], axis=1
        )
        below = (
            jnp.arange(tokens, dtype=jnp.int32)[:, None]
            > jnp.arange(tokens, dtype=jnp.int32)[None, :]
        )
        rank = jnp.where(chosen, matmul(below.astype(BF), chosen.astype(BF)), -1.0)
        rank_out = rank.T.reshape(nt * nr, nc * tokens)
        seg_out = jnp.broadcast_to(seg_ids.astype(F32), (nt * nr, group))
        tables = lax.all_to_all(
            jnp.concatenate([rank_out, seg_out], axis=1), ("tok", "row"), 0, 0
        )
        relative = jnp.arange(nt * nr, dtype=jnp.int32)
        block_order = ((relative // nr) ^ tok_i) * nr + ((relative % nr) ^ row_i)
        col_order = jnp.arange(nc, dtype=jnp.int32) ^ col_i

        def by_place(table):
            ordered = jnp.take(table, block_order, axis=0).reshape(nt * nr, nc, tokens)
            return jnp.take(ordered, col_order, axis=1)

        rank_rows = by_place(tables[:, : nc * tokens])
        rank_cols = rank_rows.transpose(0, 2, 1)

        seg_abs = lax.dynamic_slice_in_dim(tables[:, nc * tokens :], tok_i * nr, nr, 0)
        index_rel = (col_order[:, None] * tokens + jnp.arange(tokens, dtype=jnp.int32)[None, :])
        index_rel = index_rel.reshape(group)
        seg_rel = jnp.take(seg_abs.reshape(nr, nc, tokens), col_order, axis=1).reshape(nr, group)
        allowed = (seg_rel[:, :, None] == seg_rel[:, None, :]) & (
            index_rel[None, None, :] <= index_rel[None, :, None]
        )
        mask = allowed.astype(F32)
        positions = jnp.sum(mask, axis=2) - 1.0
        frequency = ROPE_BASE ** (-(jnp.arange(HD // 2, dtype=F32) * 2.0 / HD))
        angles = positions[:, :, None] * frequency[None, None, :]
        cosine = jnp.concatenate([jnp.cos(angles)] * 2, axis=2)
        sine = jnp.sin(angles)
        sine = jnp.concatenate([-sine, sine], axis=2)

        floats = hidden_in.astype(F32)
        normed = rms_scale(floats, norm1_gain).astype(BF)
        plane = plane_gather(normed)
        query_w = lax.all_to_all(w_query, "row", 1, 0, tiled=True)
        width = w_keyval.shape[1]
        keyval_cols = jnp.stack([w_keyval] + [col(w_keyval, m) for m in range(1, nc)])

        def head_block(first_col):
            return lax.dynamic_slice(
                keyval_cols,
                ((first_col // width) ^ col_i, 0, first_col % width),
                (1, w_keyval.shape[0], HD),
            )[0]

        kv_heads = [((col_i * nr + r) * heads) // group_size for r in range(nr)]
        keyval_send_w = jnp.stack(
            [
                jnp.concatenate([head_block(h * HD), head_block(key_cols + h * HD)], axis=1)
                for h in kv_heads
            ]
        )
        keyval_w = lax.all_to_all(keyval_send_w, "row", 0, 0).reshape(D, 2 * HD)
        output_w = lax.all_to_all(w_output, "row", 0, 1, tiled=True)
        normed_all = jnp.stack(plane).reshape(nc * nr * tokens, D)
        query_raw = matmul(normed_all, query_w).reshape(nc, nr, tokens, head_cols)
        keyval = matmul(normed_all, keyval_w).astype(BF).reshape(nc, nr, tokens, 2 * HD)
        qg, kg = query_gain[None], key_gain[None]
        mixed = attend(heads, query_raw, keyval, cosine, sine, mask, qg, kg)

        def by_col(values, weight):
            return [
                matmul(values[m].reshape(nr * tokens, -1), weight)
                .astype(BF)
                .reshape(nr, tokens, -1)
                for m in range(nc)
            ]

        after_attn = floats + plane_scatter(by_col(mixed, output_w))
        normed2 = rms_scale(after_attn, norm2_gain).astype(BF)

        cot_blocks = gather16(cotangent)
        row_blocks = gather16(normed2)
        logits = matmul(normed2, router)
        raised = jnp.where(chosen, jnp.exp(logits), 0.0)
        gate = raised / jnp.sum(raised, axis=1, keepdims=True)
        gate_rows = by_place(
            lax.all_to_all(gate.T.reshape(nt * nr, nc * tokens), ("tok", "row"), 0, 0)
        )
        gate_cols = gate_rows.transpose(0, 2, 1)

        def to_experts(picked):
            return jnp.concatenate([picked[0]] + [col(picked[m], m) for m in range(1, nc)])

        def from_experts(rows):
            parts = jnp.split(rows, nc)
            return [parts[0]] + [col(parts[m], m) for m in range(1, nc)]

        expert_in = to_experts(pick(row_blocks, rank_rows, capacity))
        weight_gu, weight_down = w_gate_up[0], w_down[0]
        joined = matmul(expert_in, weight_gu)
        gate_part, up_part = joined[:, :FF], joined[:, FF:]
        sigmoid_gate = jax.nn.sigmoid(gate_part)
        hidden = (gate_part * sigmoid_gate * up_part).astype(BF)
        expert_out = matmul(hidden, weight_down).astype(BF)
        mixture = reduce16(spread(from_experts(expert_out), rank_cols, capacity, gate_cols))
        layer_out = (after_attn + mixture).astype(BF)

        grad_in = to_experts(pick(cot_blocks, rank_rows, capacity, gate_rows))
        hidden_grad = contract(grad_in, weight_down, ((1,), (1,)))
        gate_back = hidden_grad * up_part * sigmoid_gate * (1.0 + gate_part * (1.0 - sigmoid_gate))
        up_back = hidden_grad * gate_part * sigmoid_gate
        joined_grad = jnp.concatenate([gate_back, up_back], axis=1).astype(BF)
        back_rows = contract(joined_grad, weight_gu, ((1,), (1,))).astype(BF)
        rows_grad = reduce16(spread(from_experts(back_rows), rank_cols, capacity))
        down_grad = contract(hidden, grad_in, ((0,), (0,)))
        gate_up_grad = contract(expert_in, joined_grad, ((0,), (0,)))

        share = jnp.sum(grad_in.astype(F32) * expert_out.astype(F32), axis=1)
        share = share.reshape(nc, nt * nr, capacity)
        share = jnp.take(jnp.take(share, col_order, axis=0), block_order, axis=1)
        share = lax.all_to_all(
            share.transpose(1, 0, 2).reshape(experts, capacity), ALL, 0, 0
        )
        slots = jnp.arange(capacity, dtype=jnp.int32).astype(F32)
        share = jnp.sum(
            jnp.where(rank[:, :, None] == slots[None, None, :], share[None], 0.0), axis=2
        )
        logit_grad = (share - gate * jnp.sum(share, axis=1, keepdims=True)).astype(BF)
        router_part = contract(normed2, logit_grad, ((0,), (0,)))
        normed2_grad = rows_grad + contract(logit_grad, router, ((1,), (1,)))

        grad_out = cotangent.astype(F32)
        _, norm2_back = jax.vjp(rms_scale, after_attn, norm2_gain)
        resid_grad, gain2_part = norm2_back(normed2_grad)
        resid_grad = resid_grad + grad_out
        out_grad = resid_grad.astype(BF)

        out_all = jnp.stack(plane_gather(out_grad)).reshape(nc * nr * tokens, D)
        mixed_grad = (
            contract(out_all, output_w, ((1,), (1,))).astype(BF).reshape(mixed.shape)
        )
        output_part = contract(mixed.reshape(-1, head_cols), out_all, ((0,), (0,)))
        output_part = output_part.reshape(nt, head_cols // nt, nr, D // nr)
        output_mine = tok_scatter(output_part, tok_i)
        output_mine = lax.all_to_all(output_mine.transpose(1, 0, 2), "row", 0, 0)
        output_block = tok_gather(output_mine, tok_i).transpose(1, 0, 2, 3)
        output_block = output_block.reshape(nr * head_cols, D // nr)

        query_send, keyval_send, qgain_part, kgain_part = attend_back(
            heads, query_raw, keyval, cosine, sine, mask, qg, kg, mixed, mixed_grad
        )
        query_flat = query_send.reshape(-1, head_cols)
        keyval_flat = keyval_send.reshape(-1, 2 * HD)

        def by_col_back(m):
            return (
                (
                    contract(query_send[m].reshape(-1, head_cols), query_w, ((1,), (1,)))
                    + contract(keyval_send[m].reshape(-1, 2 * HD), keyval_w, ((1,), (1,)))
                )
                .astype(BF)
                .reshape(nr, tokens, D)
            )

        normed_grad = plane_scatter([by_col_back(m) for m in range(nc)])
        _, norm1_back = jax.vjp(rms_scale, floats, norm1_gain)
        floats_grad, gain1_part = norm1_back(normed_grad)
        input_grad = (resid_grad + floats_grad).astype(BF)

        piece = D // nr // nt

        def reduce_rows(part):
            n = part.shape[1]
            view = part.reshape(nr, nt, piece, n).transpose(1, 0, 2, 3)
            return lax.all_to_all(tok_scatter(view, tok_i), "row", 0, 0).transpose(1, 0, 2)

        query_part = contract(normed_all, query_flat, ((0,), (0,)))
        query_mine = reduce_rows(query_part).reshape(piece, nr * head_cols)
        query_block = tok_gather(query_mine, tok_i).reshape(D // nr, nr * head_cols)

        keyval_part = contract(normed_all, keyval_flat, ((0,), (0,)))
        keyval_mine = reduce_rows(keyval_part).astype(F32)
        full = jnp.zeros((piece, 2 * key_cols), F32)
        for r in range(nr):
            for half in range(2):
                start = half * key_cols + kv_heads[r] * HD
                now = lax.dynamic_slice(full, (0, start), (piece, HD))
                new = now + keyval_mine[:, r, half * HD : (half + 1) * HD]
                full = lax.dynamic_update_slice(full, new, (0, start))
        pieces = [
            lax.dynamic_slice(full, (0, (col_i ^ m) * width), (piece, width)) for m in range(nc)
        ]
        keyval_mine = total(
            pieces[0], *[col(pieces[m].astype(BF), m) for m in range(1, nc)]
        ).astype(BF)
        keyval_block = tok_gather(keyval_mine, tok_i).reshape(D // nr, width)

        small = sum_small(
            jnp.concatenate(
                [
                    router_part.reshape(-1),
                    gain1_part,
                    gain2_part,
                    qgain_part.reshape(-1),
                    kgain_part.reshape(-1),
                ]
            )
        )
        edges = [0]
        for n in (D * experts, D, D, HD, HD):
            edges.append(edges[-1] + n)
        router_grad, norm1_grad, norm2_grad, query_gain_grad, key_gain_grad = (
            small[a:b] for a, b in zip(edges[:-1], edges[1:])
        )
        return (
            layer_out,
            input_grad,
            query_block,
            keyval_block,
            output_block,
            router_grad.reshape(D, experts),
            gate_up_grad[None],
            down_grad[None],
            norm1_grad,
            norm2_grad,
            query_gain_grad,
            key_gain_grad,
        )

    return per_device


def solution(mesh):
    by_all = P(ALL, None)
    by_expert = P(ALL, None, None)
    return jax.shard_map(
        build(dict(mesh.shape)),
        mesh=mesh,
        in_specs=(
            by_all,
            P(("tok", "row"), None),
            by_all,
            P(),
            P(),
            P(),
            P("row", "col"),
            P("row", "col"),
            P("col", "row"),
            P(),
            P(),
            by_expert,
            by_expert,
            by_all,
        ),
        out_specs=(
            by_all,
            by_all,
            P("row", "col"),
            P("row", "col"),
            P("col", "row"),
            P(),
            by_expert,
            by_expert,
            P(),
            P(),
            P(),
            P(),
        ),
        check_vma=False,
    )
```

```python
import functools
import math

import jax
import jax.numpy as jnp
from jax import lax
from jax.experimental import pallas as pl
from jax.experimental.pallas import tpu as pltpu
from jax.sharding import PartitionSpec as P


D = 2048
HQ = 32
KV = 4
HD = 128
FF = 768
TOPK = 8
EPSILON = 1e-06
ROPE_BASE = 1000000.0
BF = jnp.bfloat16
F32 = jnp.float32
ALL = ("tok", "row", "col")


def matmul(left, right):
    return jnp.dot(left, right, preferred_element_type=F32)


def contract(left, right, dims):
    return lax.dot_general(left, right, (dims, ((), ())), preferred_element_type=F32)


def rms_scale(values, gain):
    return values * lax.rsqrt(jnp.mean(values * values, axis=-1, keepdims=True) + EPSILON) * gain


def total(*parts):
    acc = parts[0].astype(F32)
    for part in parts[1:]:
        acc = acc + part.astype(F32)
    return acc


def flip(values, axis, mask, size):
    return lax.ppermute(values, axis, [(i, i ^ mask) for i in range(size)])


def estimate(flops, *arrays):
    moved = sum(math.prod(x.shape) * x.dtype.itemsize for x in arrays)
    return pl.CostEstimate(flops=flops, bytes_accessed=moved, transcendentals=0)


def turn(rows, cos_ref, sin_ref):
    return rows * cos_ref[0] + pltpu.roll(rows, HD // 2, 1) * sin_ref[0]


def turn_back(rows, cos_ref, sin_ref):
    return rows * cos_ref[0] + pltpu.roll(rows * sin_ref[0], HD // 2, 1)


def inverse_rms(rows):
    return lax.rsqrt(jnp.mean(rows * rows, axis=-1, keepdims=True) + EPSILON)


def head_of(ref, head):
    part = ref[:, 0, :, head * HD : (head + 1) * HD]
    return part.reshape(part.shape[0] * part.shape[1], HD)


def put_head(ref, head, rows):
    shape = ref.shape
    ref[:, 0, :, head * HD : (head + 1) * HD] = rows.reshape(shape[0], shape[2], HD).astype(
        ref.dtype
    )


def softmax_of(query_rows, key_rows, mask_ref):
    scores = contract(query_rows, key_rows, ((1,), (1,))) * (1.0 / math.sqrt(HD))
    raised = jnp.where(mask_ref[0] > 0.0, jnp.exp(scores), 0.0)
    return raised / jnp.sum(raised, axis=-1, keepdims=True)


def key_parts(heads, raw_ref):
    key_raw = head_of(raw_ref, heads).astype(BF).astype(F32)
    value_rows = head_of(raw_ref, heads + 1).astype(BF)
    return key_raw, value_rows


def attend_kernel(heads, raw_ref, cos_ref, sin_ref, mask_ref, qg_ref, kg_ref, out_ref):
    key_raw, value_rows = key_parts(heads, raw_ref)
    key_rows = turn(key_raw * inverse_rms(key_raw) * kg_ref[...], cos_ref, sin_ref).astype(BF)
    for head in range(heads):
        raw = head_of(raw_ref, head)
        query_rows = turn(raw * inverse_rms(raw) * qg_ref[...], cos_ref, sin_ref).astype(BF)
        attention = softmax_of(query_rows, key_rows, mask_ref).astype(BF)
        put_head(out_ref, head, contract(attention, value_rows, ((1,), (0,))))


def rms_back(raw, inverse, gain, grad):
    scaled = grad * gain
    inner = jnp.sum(scaled * raw, axis=-1, keepdims=True) * (1.0 / HD)
    raw_grad = inverse * scaled - raw * (inverse * inverse * inverse * inner)
    return raw_grad, jnp.sum(grad * raw * inverse, axis=0, keepdims=True)


def attend_back_kernel(
    heads,
    raw_ref,
    cos_ref,
    sin_ref,
    mask_ref,
    qg_ref,
    kg_ref,
    mixed_ref,
    grad_ref,
    send_ref,
    qgain_ref,
    kgain_ref,
):
    scale = 1.0 / math.sqrt(HD)
    key_raw, value_rows = key_parts(heads, raw_ref)
    key_inverse = inverse_rms(key_raw)
    key_rows = turn(key_raw * key_inverse * kg_ref[...], cos_ref, sin_ref).astype(BF)
    key_back = jnp.zeros(key_raw.shape, F32)
    value_back = jnp.zeros(key_raw.shape, F32)
    gain_sum = jnp.zeros((1, HD), F32)
    for head in range(heads):
        raw = head_of(raw_ref, head)
        inverse = inverse_rms(raw)
        query_rows = turn(raw * inverse * qg_ref[...], cos_ref, sin_ref).astype(BF)
        weights = softmax_of(query_rows, key_rows, mask_ref)
        grad = head_of(grad_ref, head)
        mixed = head_of(mixed_ref, head)
        value_back = value_back + contract(weights.astype(BF), grad, ((0,), (0,)))
        weight_grad = contract(grad, value_rows, ((1,), (1,)))
        delta = jnp.sum(grad.astype(F32) * mixed.astype(F32), axis=-1, keepdims=True)
        score_grad = (weights * (weight_grad - delta)).astype(BF)
        query_back = contract(score_grad, key_rows, ((1,), (0,))) * scale
        key_back = key_back + contract(score_grad, query_rows, ((0,), (0,))) * scale
        raw_grad, gain_part = rms_back(
            raw, inverse, qg_ref[...], turn_back(query_back, cos_ref, sin_ref)
        )
        gain_sum = gain_sum + gain_part
        put_head(send_ref, head, raw_grad)
    key_grad, kgain_part = rms_back(
        key_raw, key_inverse, kg_ref[...], turn_back(key_back, cos_ref, sin_ref)
    )
    put_head(send_ref, heads, key_grad)
    put_head(send_ref, heads + 1, value_back)

    @pl.when(pl.program_id(0) == 0)
    def _():
        qgain_ref[...] = jnp.zeros_like(qgain_ref)
        kgain_ref[...] = jnp.zeros_like(kgain_ref)

    qgain_ref[...] += gain_sum
    kgain_ref[...] += kgain_part


def group_spec(shape):
    return pl.BlockSpec((shape[0], 1) + shape[2:], lambda g: (0, g, 0, 0))


def table_spec(shape):
    return pl.BlockSpec((1,) + shape[1:], lambda g: (g, 0, 0))


def whole_spec(shape):
    return pl.BlockSpec(shape, lambda g: (0,) * len(shape))


def attention_specs(raw, cosine, sine, mask):
    return [
        group_spec(raw.shape),
        table_spec(cosine.shape),
        table_spec(sine.shape),
        table_spec(mask.shape),
        whole_spec((1, HD)),
        whole_spec((1, HD)),
    ]


def attend(heads, raw, cosine, sine, mask, qg, kg):
    shape = raw.shape[:3] + (heads * HD,)
    return pl.pallas_call(
        functools.partial(attend_kernel, heads),
        grid=(raw.shape[1],),
        in_specs=attention_specs(raw, cosine, sine, mask),
        out_specs=group_spec(shape),
        out_shape=jax.ShapeDtypeStruct(shape, BF),
        compiler_params=pltpu.CompilerParams(vmem_limit_bytes=56 << 20),
        cost_estimate=estimate(4 << 30, raw, mask),
        name="attend",
    )(raw, cosine, sine, mask, qg, kg)


def attend_back(heads, raw, cosine, sine, mask, qg, kg, mixed, grad):
    return pl.pallas_call(
        functools.partial(attend_back_kernel, heads),
        grid=(raw.shape[1],),
        in_specs=attention_specs(raw, cosine, sine, mask)
        + [group_spec(mixed.shape), group_spec(grad.shape)],
        out_specs=[
            group_spec(raw.shape),
            whole_spec((1, HD)),
            whole_spec((1, HD)),
        ],
        out_shape=[
            jax.ShapeDtypeStruct(raw.shape, BF),
            jax.ShapeDtypeStruct((1, HD), F32),
            jax.ShapeDtypeStruct((1, HD), F32),
        ],
        compiler_params=pltpu.CompilerParams(vmem_limit_bytes=56 << 20),
        cost_estimate=estimate(6 << 30, raw, raw, mask),
        name="attend_back",
    )(raw, cosine, sine, mask, qg, kg, mixed, grad)


def pick_kernel(counts, experts, capacity, scaled, *refs):
    pieces = refs[: len(counts)]
    rank_ref = refs[len(counts)]
    weight_ref = refs[len(counts) + 1] if scaled else None
    outs = refs[len(counts) + 1 + scaled : -2]
    select_ref, level_ref = refs[-2:]
    blocks, rows = rank_ref.shape[0], rank_ref.shape[2]
    places = [(p, i * rows) for p, count in enumerate(counts) for i in range(count)]
    slots = lax.broadcasted_iota(jnp.int32, (capacity, rows), 0).astype(F32)
    for block in range(blocks):
        for e in range(experts):
            hit = (slots == rank_ref[block, e : e + 1, :]).astype(F32)
            span = slice(e * capacity, (e + 1) * capacity)
            select_ref[block, span, :] = hit.astype(BF)
            if scaled:
                level = jnp.sum(hit * weight_ref[block, e : e + 1, :], axis=1, keepdims=True)
                level_ref[block, span, :] = jnp.broadcast_to(level, (capacity, 128))
    chunk = 256

    def body(step, carry):
        cols = pl.ds(pl.multiple_of(step * chunk, chunk), chunk)
        for block, (p, start) in enumerate(places):
            picked = matmul(select_ref[block], pieces[p][start : start + rows, cols])
            if scaled:
                picked = picked * jnp.concatenate([level_ref[block]] * (chunk // 128), axis=1)
            picked = picked.astype(BF)
            for e in range(experts):
                outs[e][block * capacity : (block + 1) * capacity, cols] = picked[
                    e * capacity : (e + 1) * capacity
                ]
        return carry

    lax.fori_loop(0, pieces[0].shape[1] // chunk, body, 0)


def pick(pieces, rank, capacity, weight=None):
    blocks, experts, rows = rank.shape
    operands = list(pieces) + [rank] + ([] if weight is None else [weight])
    counts = [piece.shape[0] // rows for piece in pieces]
    shape = jax.ShapeDtypeStruct((blocks * capacity, pieces[0].shape[1]), BF)
    return pl.pallas_call(
        functools.partial(pick_kernel, counts, experts, capacity, int(weight is not None)),
        in_specs=[pl.BlockSpec(memory_space=pltpu.VMEM)] * len(operands),
        out_specs=[pl.BlockSpec(memory_space=pltpu.VMEM)] * experts,
        out_shape=[shape] * experts,
        scratch_shapes=[
            pltpu.VMEM((blocks, experts * capacity, rows), BF),
            pltpu.VMEM((blocks, experts * capacity, 128), F32),
        ],
        compiler_params=pltpu.CompilerParams(vmem_limit_bytes=48 << 20),
        cost_estimate=estimate(1 << 30, *operands, *operands),
    )(*operands)


def spread_kernel(experts, capacity, scaled, *refs):
    rows_refs = refs[:experts]
    rank_ref = refs[experts]
    weight_ref = refs[experts + 1] if scaled else None
    outs = refs[experts + 1 + scaled : -2]
    place_ref, level_ref = refs[-2:]
    blocks, tokens = rank_ref.shape[0], rank_ref.shape[1]
    slots = lax.broadcasted_iota(jnp.int32, (tokens, capacity), 1).astype(F32)
    for block in range(blocks):
        for e in range(experts):
            hit = (slots == rank_ref[block, :, e : e + 1]).astype(F32)
            place_ref[block, e] = hit.astype(BF)
            if scaled:
                level_ref[block, e] = jnp.broadcast_to(
                    weight_ref[block, :, e : e + 1], (tokens, 128)
                )
    chunk = 256

    def body(step, carry):
        cols = pl.ds(pl.multiple_of(step * chunk, chunk), chunk)
        for block in range(blocks):
            acc = None
            for e in range(experts):
                part = matmul(
                    place_ref[block, e],
                    rows_refs[e][block * capacity : (block + 1) * capacity, cols],
                )
                if scaled:
                    part = part * jnp.concatenate(
                        [level_ref[block, e]] * (chunk // 128), axis=1
                    )
                acc = part if acc is None else acc + part
            outs[block][:, cols] = acc.astype(BF)
        return carry

    lax.fori_loop(0, outs[0].shape[1] // chunk, body, 0)


def spread(rows, rank, capacity, weight=None):
    blocks, tokens, experts = rank.shape
    operands = list(rows) + [rank] + ([] if weight is None else [weight])
    shape = jax.ShapeDtypeStruct((tokens, rows[0].shape[1]), BF)
    return pl.pallas_call(
        functools.partial(spread_kernel, experts, capacity, int(weight is not None)),
        in_specs=[pl.BlockSpec(memory_space=pltpu.VMEM)] * len(operands),
        out_specs=[pl.BlockSpec(memory_space=pltpu.VMEM)] * blocks,
        out_shape=[shape] * blocks,
        scratch_shapes=[
            pltpu.VMEM((blocks, experts, tokens, capacity), BF),
            pltpu.VMEM((blocks, experts, tokens, 128), F32),
        ],
        compiler_params=pltpu.CompilerParams(vmem_limit_bytes=48 << 20),
        cost_estimate=estimate(1 << 30, *operands, *operands),
    )(*operands)


def expert_kernel(x_ref, d_ref, w_ref, hidden_ref, joined_ref, back_ref):
    joined = matmul(x_ref[...], w_ref[...])
    gate, up = joined[:, :FF], joined[:, FF:]
    level = jax.nn.sigmoid(gate)
    active = gate * level
    grad = d_ref[...]
    hidden_ref[...] = (active * up).astype(BF)
    gate_back = (grad * up * level * (1.0 + gate * (1.0 - level))).astype(BF)
    up_back = (grad * active).astype(BF)
    joined_grad = jnp.concatenate([gate_back, up_back], axis=1)
    joined_ref[...] = joined_grad
    back_ref[...] = contract(joined_grad, w_ref[...], ((1,), (1,))).astype(BF)


def expert(rows, grad, weight):
    count = rows.shape[0]
    tile = min(256, count)

    def spec(n):
        return pl.BlockSpec((tile, n), lambda i: (i, 0))

    return pl.pallas_call(
        expert_kernel,
        grid=(count // tile,),
        in_specs=[spec(D), spec(FF), pl.BlockSpec(memory_space=pltpu.VMEM)],
        out_specs=[spec(FF), spec(2 * FF), spec(D)],
        out_shape=[
            jax.ShapeDtypeStruct((count, FF), BF),
            jax.ShapeDtypeStruct((count, 2 * FF), BF),
            jax.ShapeDtypeStruct((count, D), BF),
        ],
        compiler_params=pltpu.CompilerParams(vmem_limit_bytes=40 << 20),
        cost_estimate=estimate(2 * count * D * 4 * FF, rows, grad, weight),
    )(rows, grad, weight)


def result_kernel(hidden_ref, grad_ref, w_ref, out_ref, share_ref):
    out = matmul(hidden_ref[...], w_ref[...]).astype(BF)
    out_ref[...] = out
    share = jnp.sum(out.astype(F32) * grad_ref[...].astype(F32), axis=1, keepdims=True)
    share_ref[...] = jnp.broadcast_to(share, share_ref.shape)


def result(hidden, grad, weight):
    count = hidden.shape[0]
    tile = min(256, count)

    def spec(n):
        return pl.BlockSpec((tile, n), lambda i: (i, 0))

    out, share = pl.pallas_call(
        result_kernel,
        grid=(count // tile,),
        in_specs=[spec(FF), spec(D), pl.BlockSpec(memory_space=pltpu.VMEM)],
        out_specs=[spec(D), spec(128)],
        out_shape=[
            jax.ShapeDtypeStruct((count, D), BF),
            jax.ShapeDtypeStruct((count, 128), F32),
        ],
        compiler_params=pltpu.CompilerParams(vmem_limit_bytes=32 << 20),
        cost_estimate=estimate(2 * count * D * FF, grad, grad, weight),
    )(hidden, grad, weight)
    return out, share[:, 0]


def weight_grad_kernel(count, *refs):
    out_ref = refs[-1]
    acc = contract(refs[0][...], refs[count][...], ((0,), (0,)))
    for i in range(1, count):
        acc = acc + contract(refs[i][...], refs[count + i][...], ((0,), (0,)))
    out_ref[...] = acc


def weight_grad(lefts, rights, tile):
    count = len(lefts)
    m, n = lefts[0].shape[1], rights[0].shape[1]
    return pl.pallas_call(
        functools.partial(weight_grad_kernel, count),
        grid=(m // tile,),
        in_specs=[pl.BlockSpec((x.shape[0], tile), lambda i: (0, i)) for x in lefts]
        + [pl.BlockSpec(memory_space=pltpu.VMEM)] * count,
        out_specs=pl.BlockSpec((tile, n), lambda i: (i, 0)),
        out_shape=jax.ShapeDtypeStruct((m, n), F32),
        compiler_params=pltpu.CompilerParams(vmem_limit_bytes=48 << 20),
        cost_estimate=estimate(2 * m * n * count * lefts[0].shape[0], *rights, *rights, *lefts),
    )(*lefts, *rights)


def after(values, *others):
    return lax.optimization_barrier((values,) + others)[0]


def narrow(*parts):
    return total(*parts).astype(BF)


def build(sizes):
    nt, nr, nc = sizes["tok"], sizes["row"], sizes["col"]
    assert nt == 4 and nr == 4

    def tok(values, mask):
        return flip(values, "tok", mask, nt)

    def row(values, mask):
        return flip(values, "row", mask, nr)

    def col(values, mask):
        return flip(values, "col", mask, nc)

    def cols_of(values):
        return [values] + [col(values, m) for m in range(1, nc)]

    def plane_rows(own):
        half = own.shape[0] // 2
        ones, twos = row(own, 1), row(own, 2)
        threes = jnp.concatenate([row(twos[:half], 1), row(ones[half:], 2)])
        return [own, ones, twos, threes]

    def plane_gather(own):
        return jnp.stack(cols_of(jnp.stack(plane_rows(own))))

    def plane_scatter(parts):
        received = [col(parts[m], m) for m in range(1, nc)]
        mine = [narrow(parts[0][r], *[got[r] for got in received]) for r in range(nr)]
        half = mine[3].shape[0] // 2
        from_one = row(mine[3][:half], 1)
        from_two = row(mine[3][half:], 2)
        ones = jnp.concatenate([mine[1][:half], narrow(mine[1][half:], from_two)])
        twos = jnp.concatenate([narrow(mine[2][:half], from_one), mine[2][half:]])
        return total(mine[0], row(ones, 1), row(twos, 2))

    def gather16(own):
        base = [own, None, tok(own, 2), None]
        base[3] = tok(base[2], 1)
        base[1] = tok(after(own, base[2]), 1)
        out = {}
        prior = None
        for z in (0, 2, 3, 1):
            here = base[z] if prior is None else after(base[z], prior)
            ones, twos = row(here, 1), row(here, 2)
            threes = row(twos, 1) if z in (0, 2) else row(ones, 2)
            out[z] = [base[z], ones, twos, threes]
            prior = ones if z in (2, 3) else None
        return out

    def reduce_plane(parts, turn_at_one):
        ones, twos, threes = parts[1], parts[2], parts[3]
        if turn_at_one:
            ones = narrow(ones, row(threes, 2))
        else:
            twos = narrow(twos, row(threes, 1))
        return [parts[0], row(ones, 1), row(twos, 2)]

    def chain_tok(values):
        place = lax.axis_index("tok")
        inner = (place == 1) | (place == 2)
        inward = lax.ppermute(values, "tok", [(0, 1), (3, 2)])
        pair = lax.optimization_barrier(narrow(values, inward))
        whole = lax.optimization_barrier(narrow(pair, lax.ppermute(pair, "tok", [(1, 2), (2, 1)])))
        outward = lax.ppermute(whole, "tok", [(1, 0), (2, 3)])
        return jnp.where(inner, whole, outward).astype(F32)

    def sum_small(values):
        devices = nt * nr * nc
        length = values.shape[0]
        width = -(-length // (devices * 128)) * 128
        padded = jnp.concatenate([values, jnp.zeros((devices * width - length,), F32)])
        mine = jnp.sum(lax.all_to_all(padded.reshape(devices, width), ALL, 0, 0), axis=0)
        back = lax.all_to_all(jnp.broadcast_to(mine[None], (devices, width)), ALL, 0, 0)
        return back.reshape(-1)[:length]

    def per_device(
        hidden_in,
        seg_ids,
        expert_ids,
        norm1_gain,
        query_gain,
        key_gain,
        w_query,
        w_keyval,
        w_output,
        norm2_gain,
        router,
        w_gate_up,
        w_down,
        cotangent,
    ):
        return layer(
            hidden_in,
            seg_ids,
            expert_ids,
            norm1_gain,
            query_gain,
            key_gain,
            w_query,
            w_keyval,
            w_output,
            norm2_gain,
            router,
            w_gate_up,
            w_down,
            cotangent,
        )

    def layer(
        hidden_in,
        seg_ids,
        expert_ids,
        norm1_gain,
        query_gain,
        key_gain,
        w_query,
        w_keyval,
        w_output,
        norm2_gain,
        router,
        w_gate_up,
        w_down,
        cotangent,
    ):
        tok_i, row_i, col_i = (lax.axis_index(name) for name in ALL)
        experts = router.shape[1]
        tokens = hidden_in.shape[0]
        capacity = max(2, 2 * tokens * TOPK // experts)
        heads = HQ // (nr * nc)
        group_size = HQ // KV
        head_cols = heads * HD
        group = seg_ids.shape[1]
        key_cols = KV * HD
        all_cols = head_cols + 2 * HD
        row_block = D // nr
        width = w_keyval.shape[1]

        floats = hidden_in.astype(F32)
        normed = rms_scale(floats, norm1_gain).astype(BF)
        plane_norm = plane_rows(normed)
        keyval_cols = jnp.stack(cols_of(w_keyval))

        def head_block(first_col):
            return lax.dynamic_slice(
                keyval_cols,
                ((first_col // width) ^ col_i, 0, first_col % width),
                (1, row_block, HD),
            )[0]

        kv_heads = [((col_i * nr + (row_i ^ m)) * heads) // group_size for m in range(nr)]

        def weight_message(m):
            query_cols = lax.dynamic_slice_in_dim(w_query, (row_i ^ m) * head_cols, head_cols, 1)
            first = kv_heads[m] * HD
            return jnp.concatenate(
                [query_cols, head_block(first), head_block(key_cols + first)], axis=1
            )

        weight_qkv = jnp.zeros((D, all_cols), BF)
        for m in (3, 1, 2, 0):
            message = weight_message(m)
            message = row(message, m) if m else message
            weight_qkv = lax.dynamic_update_slice(
                weight_qkv, message, ((row_i ^ m) * row_block, 0)
            )
        seg_rows = seg_ids.astype(F32)
        seg_rel = jnp.concatenate([seg_rows] + [row(seg_rows, m) for m in range(1, nr)])
        col_order = jnp.arange(nc, dtype=jnp.int32) ^ col_i
        index_rel = col_order[:, None] * tokens + jnp.arange(tokens, dtype=jnp.int32)[None, :]
        index_rel = index_rel.reshape(group)
        seg_rel = jnp.take(seg_rel.reshape(nr, nc, tokens), col_order, axis=1).reshape(nr, group)
        allowed = (seg_rel[:, :, None] == seg_rel[:, None, :]) & (
            index_rel[None, None, :] <= index_rel[None, :, None]
        )
        mask = allowed.astype(F32)
        positions = jnp.sum(mask, axis=2) - 1.0
        frequency = ROPE_BASE ** (-(jnp.arange(HD // 2, dtype=F32) * 2.0 / HD))
        angles = positions[:, :, None] * frequency[None, None, :]
        cosine = jnp.concatenate([jnp.cos(angles)] * 2, axis=2)
        sine = jnp.sin(angles)
        sine = jnp.concatenate([-sine, sine], axis=2)

        chosen = jnp.any(
            expert_ids[:, :, None] == jnp.arange(experts, dtype=jnp.int32)[None, None, :], axis=1
        )
        below = (
            jnp.arange(tokens, dtype=jnp.int32)[:, None]
            > jnp.arange(tokens, dtype=jnp.int32)[None, :]
        )
        rank = jnp.where(chosen, matmul(below.astype(BF), chosen.astype(BF)), -1.0)
        relative = jnp.arange(nt * nr, dtype=jnp.int32)
        block_order = ((relative // nr) ^ tok_i) * nr + ((relative % nr) ^ row_i)

        def by_place(table):
            sent = table.T.reshape(nt * nr, nc * tokens)
            got = lax.all_to_all(sent, ("tok", "row"), 0, 0)
            got = jnp.take(got, block_order, axis=0).reshape(nt, nr, nc, tokens)
            return jnp.take(got, col_order, axis=2)

        rank_rows = by_place(after(rank, *plane_norm))
        rank_cols = rank_rows.transpose(0, 1, 3, 2)

        normed_all = jnp.stack(cols_of(jnp.stack(plane_norm))).reshape(nc * nr * tokens, D)
        raw = matmul(after(normed_all, mask, cosine, sine), weight_qkv).reshape(nc, nr, tokens, all_cols)

        cot_plane = plane_rows(cotangent)
        cot_two = [tok(part, 2) for part in cot_plane]
        cot_planes = {
            0: cot_plane,
            1: [tok(part, 1) for part in cot_plane],
            2: cot_two,
            3: [tok(part, 1) for part in cot_two],
        }

        qg, kg = query_gain[None], key_gain[None]
        mixed = attend(heads, raw, cosine, sine, mask, qg, kg)
        weight_out = jnp.zeros((head_cols, D), BF)
        for m in (3, 1, 2, 0):
            message = lax.dynamic_slice_in_dim(w_output, (row_i ^ m) * head_cols, head_cols, 0)
            message = after(row(message, m), mixed) if m else message
            weight_out = lax.dynamic_update_slice(
                weight_out, message, (0, (row_i ^ m) * row_block)
            )

        def by_col(values, weight, dims):
            return [
                contract(values[m].reshape(nr * tokens, -1), weight, dims)
                .astype(BF)
                .reshape(nr, tokens, -1)
                for m in range(nc)
            ]

        after_attn = floats + plane_scatter(by_col(mixed, weight_out, ((1,), (0,))))
        normed2 = rms_scale(after_attn, norm2_gain).astype(BF)
        row_planes = gather16(normed2)

        logits = matmul(normed2, router)
        raised = jnp.where(chosen, jnp.exp(logits), 0.0)
        gate = raised / jnp.sum(raised, axis=1, keepdims=True)
        gate_rows = by_place(gate)
        gate_cols = gate_rows.transpose(0, 1, 3, 2)

        def of_planes(table, planes):
            return jnp.concatenate([table[z] for z in planes])

        weight_gu, weight_down = w_gate_up[0], w_down[0]
        groups = ((2, 3), (0, 1))

        def exchange(picked):
            return [picked[0]] + [col(picked[m], m) for m in range(1, nc)]

        grad_in, hidden_grad = [], []
        for planes in groups:
            picked = exchange(
                pick(
                    [block for z in planes for block in cot_planes[z]],
                    of_planes(rank_rows, planes),
                    capacity,
                    of_planes(gate_rows, planes),
                ),
            )
            grad_in.append(picked)
            hidden_grad.append([contract(g, weight_down, ((1,), (1,))) for g in picked])

        expert_in, hidden, joined_grad, back = [], [], [], []
        share, mix = {}, []
        for i, planes in enumerate(groups):
            picked = exchange(
                pick(
                    after(
                        tuple(block for z in planes for block in row_planes[z]), *hidden_grad[i]
                    ),
                    of_planes(rank_rows, planes),
                    capacity,
                ),
            )
            expert_in.append(picked)
            hid, joined, results = [], [], []
            for m in range(nc):
                h, j, b = expert(picked[m], hidden_grad[i][m], weight_gu)
                hid.append(h)
                joined.append(j)
                results.append(b)
            hidden.append(hid)
            joined_grad.append(joined)
            back.append(spread(exchange(results), of_planes(rank_cols, planes), capacity))
            outs = []
            for m in range(nc):
                out, sums = result(after(hid[m], results[-1]), grad_in[i][m], weight_down)
                outs.append(out)
                for k, z in enumerate(planes):
                    share[m, z] = sums.reshape(len(planes), nr, capacity)[k]
            mix.append(
                spread(
                    exchange(outs),
                    of_planes(rank_cols, planes),
                    capacity,
                    of_planes(gate_cols, planes),
                )
            )

        far, near = back
        plane_two = reduce_plane(far[:4], False)
        plane_three = narrow(*reduce_plane(far[4:], True))
        plane_two = narrow(*plane_two, tok(plane_three, 1))
        plane_zero = reduce_plane(near[:4], False)
        plane_one = narrow(*reduce_plane(near[4:], True))
        rows_grad = total(*plane_zero, tok(plane_two, 2), tok(plane_one, 1))

        lefts = [x for part in expert_in for x in part]
        rights = [x for part in joined_grad for x in part]
        gate_up_grad = weight_grad(lefts, rights, 256)
        lefts = [x for part in hidden for x in part]
        rights = [x for part in grad_in for x in part]
        down_grad = weight_grad(lefts, rights, 256)

        share = jnp.stack([jnp.stack([share[m, z] for m in range(nc)], 1) for z in range(nt)])
        share = share.reshape(nt * nr, nc, capacity)
        share = jnp.take(jnp.take(share, block_order, axis=0), col_order, axis=1)
        share = lax.all_to_all(share.reshape(experts, capacity), ALL, 0, 0)
        slots = jnp.arange(capacity, dtype=jnp.int32).astype(F32)
        share = jnp.sum(
            jnp.where(rank[:, :, None] == slots[None, None, :], share[None], 0.0), axis=2
        )
        logit_grad = (share - gate * jnp.sum(share, axis=1, keepdims=True)).astype(BF)
        router_part = contract(normed2, logit_grad, ((0,), (0,)))
        normed2_grad = rows_grad + contract(logit_grad, router, ((1,), (1,)))

        grad_out = cotangent.astype(F32)
        _, norm2_back = jax.vjp(rms_scale, after_attn, norm2_gain)
        resid_grad, gain2_part = norm2_back(normed2_grad)
        resid_grad = resid_grad + grad_out
        out_grad = resid_grad.astype(BF)

        out_all = plane_gather(out_grad).reshape(nc * nr * tokens, D)
        mixed_grad = (
            contract(out_all, weight_out, ((1,), (1,))).astype(BF).reshape(mixed.shape)
        )
        output_part = contract(mixed.reshape(-1, head_cols), out_all, ((0,), (0,)))
        output_block = jnp.zeros((nr * head_cols, row_block), F32)
        for m in (0, 1, 2, 3):
            message = lax.dynamic_slice_in_dim(
                output_part, (row_i ^ m) * row_block, row_block, 1
            ).astype(BF)
            message = row(message, m) if m else message
            summed = chain_tok(message)
            output_block = lax.dynamic_update_slice(
                output_block, summed, ((row_i ^ m) * head_cols, 0)
            )

        qkv_send, qgain_part, kgain_part = attend_back(
            heads, raw, cosine, sine, mask, qg, kg, mixed, mixed_grad
        )
        normed_grad = plane_scatter(by_col(qkv_send, weight_qkv, ((1,), (1,))))
        _, norm1_back = jax.vjp(rms_scale, floats, norm1_gain)
        floats_grad, gain1_part = norm1_back(normed_grad)
        input_grad = (resid_grad + floats_grad).astype(BF)

        qkv_part = contract(normed_all, qkv_send.reshape(-1, all_cols), ((0,), (0,)))
        query_block = jnp.zeros((row_block, nr * head_cols), F32)
        full = jnp.zeros((row_block, 2 * key_cols), F32)
        for m in (0, 1, 2, 3):
            message = lax.dynamic_slice_in_dim(
                qkv_part, (row_i ^ m) * row_block, row_block, 0
            ).astype(BF)
            message = row(message, m) if m else message
            summed = chain_tok(message[:, :head_cols])
            query_block = lax.dynamic_update_slice(
                query_block, summed, (0, (row_i ^ m) * head_cols)
            )
            for half in range(2):
                start = half * key_cols + kv_heads[m] * HD
                first = head_cols + half * HD
                now = lax.dynamic_slice(full, (0, start), (row_block, HD))
                new = now + message[:, first : first + HD].astype(F32)
                full = lax.dynamic_update_slice(full, new, (0, start))
        pieces = [
            lax.dynamic_slice(full, (0, (col_i ^ m) * width), (row_block, width))
            for m in range(nc)
        ]
        keyval_mine = narrow(pieces[0], *[col(pieces[m].astype(BF), m) for m in range(1, nc)])
        keyval_block = chain_tok(keyval_mine)

        mix_three = narrow(*reduce_plane(mix[0][4:], True))
        mix_two = narrow(*reduce_plane(mix[0][:4], False), tok(mix_three, 1))
        mix_two = tok(mix_two, 2)
        late = [after(part, normed_grad) for part in mix[1]]
        mix_one = narrow(*reduce_plane(late[4:], True))
        mixture = total(
            *reduce_plane(late[:4], False), after(mix_two, normed_grad), tok(mix_one, 1)
        )
        layer_out = (after_attn + mixture).astype(BF)

        small = sum_small(
            jnp.concatenate(
                [
                    router_part.reshape(-1),
                    gain1_part,
                    gain2_part,
                    qgain_part.reshape(-1),
                    kgain_part.reshape(-1),
                ]
            )
        )
        edges = [0]
        for n in (D * experts, D, D, HD, HD):
            edges.append(edges[-1] + n)
        router_grad, norm1_grad, norm2_grad, query_gain_grad, key_gain_grad = (
            small[a:b] for a, b in zip(edges[:-1], edges[1:])
        )
        return (
            layer_out,
            input_grad,
            query_block,
            keyval_block,
            output_block,
            router_grad.reshape(D, experts),
            gate_up_grad[None],
            down_grad[None],
            norm1_grad,
            norm2_grad,
            query_gain_grad,
            key_gain_grad,
        )

    return per_device


def solution(mesh):
    by_all = P(ALL, None)
    by_expert = P(ALL, None, None)
    return jax.shard_map(
        build(dict(mesh.shape)),
        mesh=mesh,
        in_specs=(
            by_all,
            P(("tok", "row"), None),
            by_all,
            P(),
            P(),
            P(),
            P("row", "col"),
            P("row", "col"),
            P("col", "row"),
            P(),
            P(),
            by_expert,
            by_expert,
            by_all,
        ),
        out_specs=(
            by_all,
            by_all,
            P("row", "col"),
            P("row", "col"),
            P("col", "row"),
            P(),
            by_expert,
            by_expert,
            P(),
            P(),
            P(),
            P(),
        ),
        check_vma=False,
    )
```

```python
import functools
import math

import jax
import jax.numpy as jnp
from jax import lax
from jax.experimental import pallas as pl
from jax.experimental.pallas import tpu as pltpu
from jax.sharding import PartitionSpec as P


D = 2048
HQ = 32
KV = 4
HD = 128
FF = 768
TOPK = 8
EPSILON = 1e-06
ROPE_BASE = 1000000.0
BF = jnp.bfloat16
F32 = jnp.float32
ALL = ("tok", "row", "col")


def matmul(left, right):
    return jnp.dot(left, right, preferred_element_type=F32)


def contract(left, right, dims):
    return lax.dot_general(left, right, (dims, ((), ())), preferred_element_type=F32)


def rms_scale(values, gain):
    return values * lax.rsqrt(jnp.mean(values * values, axis=-1, keepdims=True) + EPSILON) * gain


def total(*parts):
    acc = parts[0].astype(F32)
    for part in parts[1:]:
        acc = acc + part.astype(F32)
    return acc


def flip(values, axis, mask, size):
    return lax.ppermute(values, axis, [(i, i ^ mask) for i in range(size)])


def estimate(flops, *arrays):
    moved = sum(math.prod(x.shape) * x.dtype.itemsize for x in arrays)
    return pl.CostEstimate(flops=flops, bytes_accessed=moved, transcendentals=0)


def turn(rows, cos_ref, sin_ref):
    return rows * cos_ref[0] + pltpu.roll(rows, HD // 2, 1) * sin_ref[0]


def turn_back(rows, cos_ref, sin_ref):
    return rows * cos_ref[0] + pltpu.roll(rows * sin_ref[0], HD // 2, 1)


def inverse_rms(rows):
    return lax.rsqrt(jnp.mean(rows * rows, axis=-1, keepdims=True) + EPSILON)


def head_of(ref, head):
    part = ref[:, 0, :, head * HD : (head + 1) * HD]
    return part.reshape(part.shape[0] * part.shape[1], HD)


def put_head(ref, head, rows):
    shape = ref.shape
    ref[:, 0, :, head * HD : (head + 1) * HD] = rows.reshape(shape[0], shape[2], HD).astype(
        ref.dtype
    )


def softmax_of(query_rows, key_rows, mask_ref):
    scores = contract(query_rows, key_rows, ((1,), (1,)))
    raised = jnp.exp2(scores * (math.log2(math.e) / math.sqrt(HD))) * mask_ref[0]
    return raised * (1.0 / jnp.sum(raised, axis=-1, keepdims=True))


def key_parts(heads, raw_ref):
    key_raw = head_of(raw_ref, heads).astype(BF).astype(F32)
    value_rows = head_of(raw_ref, heads + 1).astype(BF)
    return key_raw, value_rows


def attend_kernel(heads, raw_ref, cos_ref, sin_ref, mask_ref, qg_ref, kg_ref, out_ref):
    key_raw, value_rows = key_parts(heads, raw_ref)
    key_rows = turn(key_raw * inverse_rms(key_raw) * kg_ref[...], cos_ref, sin_ref).astype(BF)
    for head in range(heads):
        raw = head_of(raw_ref, head)
        query_rows = turn(raw * inverse_rms(raw) * qg_ref[...], cos_ref, sin_ref).astype(BF)
        attention = softmax_of(query_rows, key_rows, mask_ref).astype(BF)
        put_head(out_ref, head, contract(attention, value_rows, ((1,), (0,))))


def rms_back(raw, inverse, gain, grad):
    scaled = grad * gain
    inner = jnp.sum(scaled * raw, axis=-1, keepdims=True) * (1.0 / HD)
    raw_grad = inverse * scaled - raw * (inverse * inverse * inverse * inner)
    return raw_grad, jnp.sum(grad * raw * inverse, axis=0, keepdims=True)


def attend_back_kernel(
    heads,
    raw_ref,
    cos_ref,
    sin_ref,
    mask_ref,
    qg_ref,
    kg_ref,
    mixed_ref,
    grad_ref,
    send_ref,
    qgain_ref,
    kgain_ref,
):
    scale = 1.0 / math.sqrt(HD)
    key_raw, value_rows = key_parts(heads, raw_ref)
    key_inverse = inverse_rms(key_raw)
    key_rows = turn(key_raw * key_inverse * kg_ref[...], cos_ref, sin_ref).astype(BF)
    key_back = jnp.zeros(key_raw.shape, F32)
    value_back = jnp.zeros(key_raw.shape, F32)
    gain_sum = jnp.zeros((1, HD), F32)
    for head in range(heads):
        raw = head_of(raw_ref, head)
        inverse = inverse_rms(raw)
        query_rows = turn(raw * inverse * qg_ref[...], cos_ref, sin_ref).astype(BF)
        weights = softmax_of(query_rows, key_rows, mask_ref)
        grad = head_of(grad_ref, head)
        mixed = head_of(mixed_ref, head)
        value_back = value_back + contract(weights.astype(BF), grad, ((0,), (0,)))
        weight_grad = contract(grad, value_rows, ((1,), (1,)))
        delta = jnp.sum(grad.astype(F32) * mixed.astype(F32), axis=-1, keepdims=True)
        score_grad = (weights * (weight_grad - delta)).astype(BF)
        query_back = contract(score_grad, key_rows, ((1,), (0,))) * scale
        key_back = key_back + contract(score_grad, query_rows, ((0,), (0,))) * scale
        raw_grad, gain_part = rms_back(
            raw, inverse, qg_ref[...], turn_back(query_back, cos_ref, sin_ref)
        )
        gain_sum = gain_sum + gain_part
        put_head(send_ref, head, raw_grad)
    key_grad, kgain_part = rms_back(
        key_raw, key_inverse, kg_ref[...], turn_back(key_back, cos_ref, sin_ref)
    )
    put_head(send_ref, heads, key_grad)
    put_head(send_ref, heads + 1, value_back)

    @pl.when(pl.program_id(0) == 0)
    def _():
        qgain_ref[...] = jnp.zeros_like(qgain_ref)
        kgain_ref[...] = jnp.zeros_like(kgain_ref)

    qgain_ref[...] += gain_sum
    kgain_ref[...] += kgain_part


def group_spec(shape):
    return pl.BlockSpec((shape[0], 1) + shape[2:], lambda g: (0, g, 0, 0))


def table_spec(shape):
    return pl.BlockSpec((1,) + shape[1:], lambda g: (g, 0, 0))


def whole_spec(shape):
    return pl.BlockSpec(shape, lambda g: (0,) * len(shape))


def attention_specs(raw, cosine, sine, mask):
    return [
        group_spec(raw.shape),
        table_spec(cosine.shape),
        table_spec(sine.shape),
        table_spec(mask.shape),
        whole_spec((1, HD)),
        whole_spec((1, HD)),
    ]


def attend(heads, raw, cosine, sine, mask, qg, kg):
    shape = raw.shape[:3] + (heads * HD,)
    return pl.pallas_call(
        functools.partial(attend_kernel, heads),
        grid=(raw.shape[1],),
        in_specs=attention_specs(raw, cosine, sine, mask),
        out_specs=group_spec(shape),
        out_shape=jax.ShapeDtypeStruct(shape, BF),
        compiler_params=pltpu.CompilerParams(vmem_limit_bytes=56 << 20),
        cost_estimate=estimate(4 << 30, raw, mask),
        name="attend",
    )(raw, cosine, sine, mask, qg, kg)


def attend_back(heads, raw, cosine, sine, mask, qg, kg, mixed, grad):
    return pl.pallas_call(
        functools.partial(attend_back_kernel, heads),
        grid=(raw.shape[1],),
        in_specs=attention_specs(raw, cosine, sine, mask)
        + [group_spec(mixed.shape), group_spec(grad.shape)],
        out_specs=[
            group_spec(raw.shape),
            whole_spec((1, HD)),
            whole_spec((1, HD)),
        ],
        out_shape=[
            jax.ShapeDtypeStruct(raw.shape, BF),
            jax.ShapeDtypeStruct((1, HD), F32),
            jax.ShapeDtypeStruct((1, HD), F32),
        ],
        compiler_params=pltpu.CompilerParams(vmem_limit_bytes=56 << 20),
        cost_estimate=estimate(6 << 30, raw, raw, mask),
        name="attend_back",
    )(raw, cosine, sine, mask, qg, kg, mixed, grad)


def pick_kernel(counts, experts, capacity, scaled, *refs):
    pieces = refs[: len(counts)]
    rank_ref = refs[len(counts)]
    weight_ref = refs[len(counts) + 1] if scaled else None
    outs = refs[len(counts) + 1 + scaled : -2]
    select_ref, level_ref = refs[-2:]
    blocks, rows = rank_ref.shape[0], rank_ref.shape[2]
    places = [(p, i * rows) for p, count in enumerate(counts) for i in range(count)]
    slots = lax.broadcasted_iota(jnp.int32, (capacity, rows), 0).astype(F32)
    for block in range(blocks):
        for e in range(experts):
            hit = (slots == rank_ref[block, e : e + 1, :]).astype(F32)
            span = slice(e * capacity, (e + 1) * capacity)
            select_ref[block, span, :] = hit.astype(BF)
            if scaled:
                level = jnp.sum(hit * weight_ref[block, e : e + 1, :], axis=1, keepdims=True)
                level_ref[block, span, :] = jnp.broadcast_to(level, (capacity, 128))
    chunk = 256

    def body(step, carry):
        cols = pl.ds(pl.multiple_of(step * chunk, chunk), chunk)
        for block, (p, start) in enumerate(places):
            picked = matmul(select_ref[block], pieces[p][start : start + rows, cols])
            if scaled:
                picked = picked * jnp.concatenate([level_ref[block]] * (chunk // 128), axis=1)
            picked = picked.astype(BF)
            for e in range(experts):
                outs[e][block * capacity : (block + 1) * capacity, cols] = picked[
                    e * capacity : (e + 1) * capacity
                ]
        return carry

    lax.fori_loop(0, pieces[0].shape[1] // chunk, body, 0)


def pick(pieces, rank, capacity, weight=None):
    blocks, experts, rows = rank.shape
    operands = list(pieces) + [rank] + ([] if weight is None else [weight])
    counts = [piece.shape[0] // rows for piece in pieces]
    shape = jax.ShapeDtypeStruct((blocks * capacity, pieces[0].shape[1]), BF)
    return pl.pallas_call(
        functools.partial(pick_kernel, counts, experts, capacity, int(weight is not None)),
        in_specs=[pl.BlockSpec(memory_space=pltpu.VMEM)] * len(operands),
        out_specs=[pl.BlockSpec(memory_space=pltpu.VMEM)] * experts,
        out_shape=[shape] * experts,
        scratch_shapes=[
            pltpu.VMEM((blocks, experts * capacity, rows), BF),
            pltpu.VMEM((blocks, experts * capacity, 128), F32),
        ],
        compiler_params=pltpu.CompilerParams(vmem_limit_bytes=48 << 20),
        cost_estimate=estimate(1 << 30, *operands, *operands),
    )(*operands)


def spread_kernel(experts, capacity, scaled, *refs):
    rows_refs = refs[:experts]
    rank_ref = refs[experts]
    weight_ref = refs[experts + 1] if scaled else None
    outs = refs[experts + 1 + scaled : -2]
    place_ref, level_ref = refs[-2:]
    blocks, tokens = rank_ref.shape[0], rank_ref.shape[1]
    slots = lax.broadcasted_iota(jnp.int32, (tokens, capacity), 1).astype(F32)
    for block in range(blocks):
        for e in range(experts):
            hit = (slots == rank_ref[block, :, e : e + 1]).astype(F32)
            place_ref[block, e] = hit.astype(BF)
            if scaled:
                level_ref[block, e] = jnp.broadcast_to(
                    weight_ref[block, :, e : e + 1], (tokens, 128)
                )
    chunk = 256

    def body(step, carry):
        cols = pl.ds(pl.multiple_of(step * chunk, chunk), chunk)
        for block in range(blocks):
            acc = None
            for e in range(experts):
                part = matmul(
                    place_ref[block, e],
                    rows_refs[e][block * capacity : (block + 1) * capacity, cols],
                )
                if scaled:
                    part = part * jnp.concatenate(
                        [level_ref[block, e]] * (chunk // 128), axis=1
                    )
                acc = part if acc is None else acc + part
            outs[block][:, cols] = acc.astype(BF)
        return carry

    lax.fori_loop(0, outs[0].shape[1] // chunk, body, 0)


def spread(rows, rank, capacity, weight=None):
    blocks, tokens, experts = rank.shape
    operands = list(rows) + [rank] + ([] if weight is None else [weight])
    shape = jax.ShapeDtypeStruct((tokens, rows[0].shape[1]), BF)
    return pl.pallas_call(
        functools.partial(spread_kernel, experts, capacity, int(weight is not None)),
        in_specs=[pl.BlockSpec(memory_space=pltpu.VMEM)] * len(operands),
        out_specs=[pl.BlockSpec(memory_space=pltpu.VMEM)] * blocks,
        out_shape=[shape] * blocks,
        scratch_shapes=[
            pltpu.VMEM((blocks, experts, tokens, capacity), BF),
            pltpu.VMEM((blocks, experts, tokens, 128), F32),
        ],
        compiler_params=pltpu.CompilerParams(vmem_limit_bytes=48 << 20),
        cost_estimate=estimate(1 << 30, *operands, *operands),
    )(*operands)


def expert_kernel(x_ref, d_ref, w_ref, hidden_ref, joined_ref, back_ref):
    joined = matmul(x_ref[...], w_ref[...])
    gate, up = joined[:, :FF], joined[:, FF:]
    level = jax.nn.sigmoid(gate)
    active = gate * level
    grad = d_ref[...]
    hidden_ref[...] = (active * up).astype(BF)
    gate_back = (grad * up * level * (1.0 + gate * (1.0 - level))).astype(BF)
    up_back = (grad * active).astype(BF)
    joined_grad = jnp.concatenate([gate_back, up_back], axis=1)
    joined_ref[...] = joined_grad
    back_ref[...] = contract(joined_grad, w_ref[...], ((1,), (1,))).astype(BF)


def expert(rows, grad, weight):
    count = rows.shape[0]
    tile = min(256, count)

    def spec(n):
        return pl.BlockSpec((tile, n), lambda i: (i, 0))

    return pl.pallas_call(
        expert_kernel,
        grid=(count // tile,),
        in_specs=[spec(D), spec(FF), pl.BlockSpec(memory_space=pltpu.VMEM)],
        out_specs=[spec(FF), spec(2 * FF), spec(D)],
        out_shape=[
            jax.ShapeDtypeStruct((count, FF), BF),
            jax.ShapeDtypeStruct((count, 2 * FF), BF),
            jax.ShapeDtypeStruct((count, D), BF),
        ],
        compiler_params=pltpu.CompilerParams(vmem_limit_bytes=40 << 20),
        cost_estimate=estimate(2 * count * D * 4 * FF, rows, grad, weight),
    )(rows, grad, weight)


def result_kernel(hidden_ref, grad_ref, w_ref, out_ref, share_ref):
    out = matmul(hidden_ref[...], w_ref[...]).astype(BF)
    out_ref[...] = out
    share = jnp.sum(out.astype(F32) * grad_ref[...].astype(F32), axis=1, keepdims=True)
    share_ref[...] = jnp.broadcast_to(share, share_ref.shape)


def result(hidden, grad, weight):
    count = hidden.shape[0]
    tile = min(256, count)

    def spec(n):
        return pl.BlockSpec((tile, n), lambda i: (i, 0))

    out, share = pl.pallas_call(
        result_kernel,
        grid=(count // tile,),
        in_specs=[spec(FF), spec(D), pl.BlockSpec(memory_space=pltpu.VMEM)],
        out_specs=[spec(D), spec(128)],
        out_shape=[
            jax.ShapeDtypeStruct((count, D), BF),
            jax.ShapeDtypeStruct((count, 128), F32),
        ],
        compiler_params=pltpu.CompilerParams(vmem_limit_bytes=32 << 20),
        cost_estimate=estimate(2 * count * D * FF, grad, grad, weight),
    )(hidden, grad, weight)
    return out, share[:, 0]


def weight_grad_kernel(count, *refs):
    out_ref = refs[-1]
    acc = contract(refs[0][...], refs[count][...], ((0,), (0,)))
    for i in range(1, count):
        acc = acc + contract(refs[i][...], refs[count + i][...], ((0,), (0,)))
    out_ref[...] = acc


def weight_grad(lefts, rights, tile):
    count = len(lefts)
    m, n = lefts[0].shape[1], rights[0].shape[1]
    return pl.pallas_call(
        functools.partial(weight_grad_kernel, count),
        grid=(m // tile,),
        in_specs=[pl.BlockSpec((x.shape[0], tile), lambda i: (0, i)) for x in lefts]
        + [pl.BlockSpec(memory_space=pltpu.VMEM)] * count,
        out_specs=pl.BlockSpec((tile, n), lambda i: (i, 0)),
        out_shape=jax.ShapeDtypeStruct((m, n), F32),
        compiler_params=pltpu.CompilerParams(vmem_limit_bytes=48 << 20),
        cost_estimate=estimate(2 * m * n * count * lefts[0].shape[0], *rights, *rights, *lefts),
    )(*lefts, *rights)


def kv_columns_kernel(heads_sm, *refs):
    out_ref = refs[-1]
    rows = out_ref.shape[0]
    for side in range(2):
        for head in range(KV):
            acc = jnp.zeros((rows, HD), F32)
            for m, ref in enumerate(refs[:-1]):
                part = ref[:, side * HD : (side + 1) * HD].astype(F32)
                acc = acc + jnp.where(heads_sm[m] == head, part, 0.0)
            out_ref[:, (side * KV + head) * HD : (side * KV + head + 1) * HD] = acc


def kv_columns(parts, kv_heads):
    rows = parts[0].shape[0]
    return pl.pallas_call(
        kv_columns_kernel,
        in_specs=[pl.BlockSpec(memory_space=pltpu.SMEM)]
        + [pl.BlockSpec(memory_space=pltpu.VMEM)] * len(parts),
        out_specs=pl.BlockSpec(memory_space=pltpu.VMEM),
        out_shape=jax.ShapeDtypeStruct((rows, 2 * KV * HD), F32),
        compiler_params=pltpu.CompilerParams(vmem_limit_bytes=16 << 20),
        cost_estimate=estimate(1 << 20, *parts, *parts),
        name="kvcols",
    )(jnp.stack(kv_heads).astype(jnp.int32), *parts)


def after(values, *others):
    return lax.optimization_barrier((values,) + others)[0]


def narrow(*parts):
    return total(*parts).astype(BF)


def build(sizes):
    nt, nr, nc = sizes["tok"], sizes["row"], sizes["col"]
    assert nt == 4 and nr == 4

    def tok(values, mask):
        return flip(values, "tok", mask, nt)

    def row(values, mask):
        return flip(values, "row", mask, nr)

    def col(values, mask):
        return flip(values, "col", mask, nc)

    def cols_of(values):
        return [values] + [col(values, m) for m in range(1, nc)]

    def plane_rows(own):
        half = own.shape[0] // 2
        ones, twos = row(own, 1), row(own, 2)
        threes = jnp.concatenate([row(twos[:half], 1), row(ones[half:], 2)])
        return [own, ones, twos, threes]

    def plane_gather(own):
        return jnp.stack(cols_of(jnp.stack(plane_rows(own))))

    def plane_scatter(parts):
        received = [col(parts[m], m) for m in range(1, nc)]
        mine = [narrow(parts[0][r], *[got[r] for got in received]) for r in range(nr)]
        half = mine[3].shape[0] // 2
        from_one = row(mine[3][:half], 1)
        from_two = row(mine[3][half:], 2)
        ones = jnp.concatenate([mine[1][:half], narrow(mine[1][half:], from_two)])
        twos = jnp.concatenate([narrow(mine[2][:half], from_one), mine[2][half:]])
        return total(mine[0], row(ones, 1), row(twos, 2))

    def gather16(own):
        base = [own, None, tok(own, 2), None]
        base[3] = tok(base[2], 1)
        base[1] = tok(after(own, base[2]), 1)
        out = {}
        prior = None
        for z in (0, 2, 3, 1):
            here = base[z] if prior is None else after(base[z], prior)
            ones, twos = row(here, 1), row(here, 2)
            threes = row(twos, 1) if z in (0, 2) else row(ones, 2)
            out[z] = [base[z], ones, twos, threes]
            prior = ones if z in (2, 3) else None
        return out

    def reduce_plane(parts, turn_at_one):
        ones, twos, threes = parts[1], parts[2], parts[3]
        if turn_at_one:
            ones = narrow(ones, row(threes, 2))
        else:
            twos = narrow(twos, row(threes, 1))
        return [parts[0], row(ones, 1), row(twos, 2)]

    def chain_tok(values):
        place = lax.axis_index("tok")
        inner = (place == 1) | (place == 2)
        inward = lax.ppermute(values, "tok", [(0, 1), (3, 2)])
        pair = lax.optimization_barrier(narrow(values, inward))
        whole = lax.optimization_barrier(narrow(pair, lax.ppermute(pair, "tok", [(1, 2), (2, 1)])))
        outward = lax.ppermute(whole, "tok", [(1, 0), (2, 3)])
        return jnp.where(inner, whole, outward).astype(F32), pair

    def sum_small(values):
        devices = nt * nr * nc
        length = values.shape[0]
        width = -(-length // (devices * 128)) * 128
        padded = jnp.concatenate([values, jnp.zeros((devices * width - length,), F32)])
        mine = jnp.sum(lax.all_to_all(padded.reshape(devices, width), ALL, 0, 0), axis=0)
        back = lax.all_to_all(jnp.broadcast_to(mine[None], (devices, width)), ALL, 0, 0)
        return back.reshape(-1)[:length]

    def per_device(
        hidden_in,
        seg_ids,
        expert_ids,
        norm1_gain,
        query_gain,
        key_gain,
        w_query,
        w_keyval,
        w_output,
        norm2_gain,
        router,
        w_gate_up,
        w_down,
        cotangent,
    ):
        return layer(
            hidden_in,
            seg_ids,
            expert_ids,
            norm1_gain,
            query_gain,
            key_gain,
            w_query,
            w_keyval,
            w_output,
            norm2_gain,
            router,
            w_gate_up,
            w_down,
            cotangent,
        )

    def layer(
        hidden_in,
        seg_ids,
        expert_ids,
        norm1_gain,
        query_gain,
        key_gain,
        w_query,
        w_keyval,
        w_output,
        norm2_gain,
        router,
        w_gate_up,
        w_down,
        cotangent,
    ):
        tok_i, row_i, col_i = (lax.axis_index(name) for name in ALL)
        experts = router.shape[1]
        tokens = hidden_in.shape[0]
        capacity = max(2, 2 * tokens * TOPK // experts)
        heads = HQ // (nr * nc)
        group_size = HQ // KV
        head_cols = heads * HD
        group = seg_ids.shape[1]
        key_cols = KV * HD
        all_cols = head_cols + 2 * HD
        row_block = D // nr
        width = w_keyval.shape[1]

        floats = hidden_in.astype(F32)
        normed = rms_scale(floats, norm1_gain).astype(BF)
        plane_norm = plane_rows(normed)
        keyval_cols = jnp.stack(cols_of(w_keyval))

        def head_block(first_col):
            return lax.dynamic_slice(
                keyval_cols,
                ((first_col // width) ^ col_i, 0, first_col % width),
                (1, row_block, HD),
            )[0]

        kv_heads = [((col_i * nr + (row_i ^ m)) * heads) // group_size for m in range(nr)]

        def weight_message(m):
            query_cols = lax.dynamic_slice_in_dim(w_query, (row_i ^ m) * head_cols, head_cols, 1)
            first = kv_heads[m] * HD
            return jnp.concatenate(
                [query_cols, head_block(first), head_block(key_cols + first)], axis=1
            )

        weight_qkv = jnp.zeros((D, all_cols), BF)
        for m in (3, 1, 2, 0):
            message = weight_message(m)
            message = row(message, m) if m else message
            weight_qkv = lax.dynamic_update_slice(
                weight_qkv, message, ((row_i ^ m) * row_block, 0)
            )
        seg_rows = seg_ids.astype(F32)
        seg_rel = jnp.concatenate([seg_rows] + [row(seg_rows, m) for m in range(1, nr)])
        col_order = jnp.arange(nc, dtype=jnp.int32) ^ col_i
        index_rel = col_order[:, None] * tokens + jnp.arange(tokens, dtype=jnp.int32)[None, :]
        index_rel = index_rel.reshape(group)
        seg_rel = jnp.take(seg_rel.reshape(nr, nc, tokens), col_order, axis=1).reshape(nr, group)
        allowed = (seg_rel[:, :, None] == seg_rel[:, None, :]) & (
            index_rel[None, None, :] <= index_rel[None, :, None]
        )
        mask = allowed.astype(F32)
        positions = jnp.sum(mask, axis=2) - 1.0
        frequency = ROPE_BASE ** (-(jnp.arange(HD // 2, dtype=F32) * 2.0 / HD))
        angles = positions[:, :, None] * frequency[None, None, :]
        cosine = jnp.concatenate([jnp.cos(angles)] * 2, axis=2)
        sine = jnp.sin(angles)
        sine = jnp.concatenate([-sine, sine], axis=2)

        plane_norm = after(jnp.stack(plane_norm), mask, cosine, sine)
        normed_all = jnp.stack(cols_of(plane_norm)).reshape(nc * nr * tokens, D)
        raw = matmul(normed_all, weight_qkv).reshape(nc, nr, tokens, all_cols)

        chosen = jnp.any(
            expert_ids[:, :, None] == jnp.arange(experts, dtype=jnp.int32)[None, None, :], axis=1
        )
        below = (
            jnp.arange(tokens, dtype=jnp.int32)[:, None]
            > jnp.arange(tokens, dtype=jnp.int32)[None, :]
        )
        rank = jnp.where(chosen, matmul(below.astype(BF), chosen.astype(BF)), -1.0)
        relative = jnp.arange(nt * nr, dtype=jnp.int32)
        block_order = ((relative // nr) ^ tok_i) * nr + ((relative % nr) ^ row_i)

        cot_plane = plane_rows(cotangent)
        cot_planes = {0: cot_plane}
        for z in (1, 2, 3):
            if z == 3:
                first, last = (tok(cot_planes[2][k], 1) for k in (0, 3))
            else:
                first, last = (tok(cot_plane[k], z) for k in (0, 3))
            cot_planes[z] = [first, row(first, 1), row(first, 2), last]

        qg, kg = query_gain[None], key_gain[None]
        mixed = attend(heads, raw, cosine, sine, mask, qg, kg)
        weight_out = jnp.zeros((head_cols, D), BF)
        for m in (3, 1, 2, 0):
            message = lax.dynamic_slice_in_dim(w_output, (row_i ^ m) * head_cols, head_cols, 0)
            message = after(row(message, m), mixed) if m else message
            weight_out = lax.dynamic_update_slice(
                weight_out, message, (0, (row_i ^ m) * row_block)
            )

        def by_col(values, weight, dims):
            return [
                contract(values[m].reshape(nr * tokens, -1), weight, dims)
                .astype(BF)
                .reshape(nr, tokens, -1)
                for m in range(nc)
            ]

        after_attn = floats + plane_scatter(by_col(mixed, weight_out, ((1,), (0,))))
        normed2 = rms_scale(after_attn, norm2_gain).astype(BF)
        row_planes = gather16(normed2)

        logits = matmul(normed2, router)
        raised = jnp.where(chosen, jnp.exp(logits), 0.0)
        gate = raised / jnp.sum(raised, axis=1, keepdims=True)
        sent = jnp.concatenate(
            [
                rank.T.reshape(nt * nr, nc * tokens),
                gate.T.reshape(nt * nr, nc * tokens),
            ],
            axis=1,
        )
        tables = lax.all_to_all(sent, ("tok", "row"), 0, 0)
        tables = after(tables, row_planes[3][0])
        tables = jnp.take(tables, block_order, axis=0).reshape(nt, nr, 2, nc, tokens)
        tables = jnp.take(tables, col_order, axis=3)
        rank_rows, gate_rows = tables[:, :, 0], tables[:, :, 1]
        rank_cols, gate_cols = (t.transpose(0, 1, 3, 2) for t in (rank_rows, gate_rows))

        def of_planes(table, planes):
            return jnp.concatenate([table[z] for z in planes])

        weight_gu, weight_down = w_gate_up[0], w_down[0]
        groups = ((2, 3), (0, 1))

        def exchange(picked):
            return [picked[0]] + [col(picked[m], m) for m in range(1, nc)]

        grad_in, hidden_grad = [], []
        for planes in groups:
            picked = exchange(
                pick(
                    [block for z in planes for block in cot_planes[z]],
                    of_planes(rank_rows, planes),
                    capacity,
                    of_planes(gate_rows, planes),
                ),
            )
            grad_in.append(picked)
            hidden_grad.append([contract(g, weight_down, ((1,), (1,))) for g in picked])

        expert_in, hidden, joined_grad, back = [], [], [], []
        share, mix = {}, []
        for i, planes in enumerate(groups):
            picked = exchange(
                pick(
                    after(
                        tuple(block for z in planes for block in row_planes[z]), *hidden_grad[0], *hidden_grad[1]
                    ),
                    of_planes(rank_rows, planes),
                    capacity,
                ),
            )
            expert_in.append(picked)
            hid, joined, results = [], [], []
            for m in range(nc):
                h, j, b = expert(picked[m], hidden_grad[i][m], weight_gu)
                hid.append(h)
                joined.append(j)
                results.append(b)
            hidden.append(hid)
            joined_grad.append(joined)
            back.append(spread(exchange(results), of_planes(rank_cols, planes), capacity))
            outs = []
            for m in range(nc):
                out, sums = result(after(hid[m], results[-1]), grad_in[i][m], weight_down)
                outs.append(out)
                for k, z in enumerate(planes):
                    share[m, z] = sums.reshape(len(planes), nr, capacity)[k]
            mix.append(
                spread(
                    exchange(outs),
                    of_planes(rank_cols, planes),
                    capacity,
                    of_planes(gate_cols, planes),
                )
            )

        far, near = back
        plane_two = reduce_plane(far[:4], False)
        plane_three = narrow(*reduce_plane(far[4:], True))
        plane_two = narrow(*plane_two, tok(plane_three, 1))
        plane_zero = reduce_plane(near[:4], False)
        plane_one = narrow(*reduce_plane(near[4:], True))
        rows_grad = total(*plane_zero, tok(plane_two, 2), tok(plane_one, 1))

        lefts = [x for part in expert_in for x in part]
        rights = [x for part in joined_grad for x in part]
        gate_up_grad = weight_grad(lefts, rights, 256)
        lefts = [x for part in hidden for x in part]
        rights = [x for part in grad_in for x in part]
        down_grad = weight_grad(lefts, rights, 256)

        share = jnp.stack([jnp.stack([share[m, z] for m in range(nc)], 1) for z in range(nt)])
        share = share.reshape(nt * nr, nc, capacity)
        share = jnp.take(jnp.take(share, block_order, axis=0), col_order, axis=1)
        share = lax.all_to_all(share.reshape(experts, capacity), ALL, 0, 0)
        slots = jnp.arange(capacity, dtype=jnp.int32).astype(F32)
        share = jnp.sum(
            jnp.where(rank[:, :, None] == slots[None, None, :], share[None], 0.0), axis=2
        )
        logit_grad = (share - gate * jnp.sum(share, axis=1, keepdims=True)).astype(BF)
        router_part = contract(normed2, logit_grad, ((0,), (0,)))
        normed2_grad = rows_grad + contract(logit_grad, router, ((1,), (1,)))

        grad_out = cotangent.astype(F32)
        _, norm2_back = jax.vjp(rms_scale, after_attn, norm2_gain)
        resid_grad, gain2_part = norm2_back(normed2_grad)
        resid_grad = resid_grad + grad_out
        out_grad = resid_grad.astype(BF)

        out_all = plane_gather(out_grad).reshape(nc * nr * tokens, D)
        mixed_grad = (
            contract(out_all, weight_out, ((1,), (1,))).astype(BF).reshape(mixed.shape)
        )
        output_part = contract(mixed.reshape(-1, head_cols), out_all, ((0,), (0,)))
        output_block = jnp.zeros((nr * head_cols, row_block), F32)
        pairs = []
        for m in (0, 1, 2, 3):
            message = lax.dynamic_slice_in_dim(
                output_part, (row_i ^ m) * row_block, row_block, 1
            ).astype(BF)
            message = row(message, m) if m else message
            summed, pair = chain_tok(message)
            pairs.append(pair)
            output_block = lax.dynamic_update_slice(
                output_block, summed, ((row_i ^ m) * head_cols, 0)
            )

        qkv_send, qgain_part, kgain_part = attend_back(
            heads, raw, cosine, sine, mask, qg, kg, mixed, mixed_grad
        )
        normed_grad = plane_scatter(by_col(qkv_send, weight_qkv, ((1,), (1,))))
        _, norm1_back = jax.vjp(rms_scale, floats, norm1_gain)
        floats_grad, gain1_part = norm1_back(normed_grad)
        input_grad = (resid_grad + floats_grad).astype(BF)

        qkv_part = contract(normed_all, qkv_send.reshape(-1, all_cols), ((0,), (0,)))
        query_block = jnp.zeros((row_block, nr * head_cols), F32)
        messages = []
        for m in (0, 1, 2, 3):
            message = lax.dynamic_slice_in_dim(
                qkv_part, (row_i ^ m) * row_block, row_block, 0
            ).astype(BF)
            if m:
                message = after(row(message, m), pairs[min(m + 1, 3)])
            messages.append(message)
            summed, _ = chain_tok(message[:, :head_cols])
            query_block = lax.dynamic_update_slice(
                query_block, summed, (0, (row_i ^ m) * head_cols)
            )
        full = kv_columns([message[:, head_cols:] for message in messages], kv_heads)
        pieces = [
            lax.dynamic_slice(full, (0, (col_i ^ m) * width), (row_block, width))
            for m in range(nc)
        ]
        keyval_mine = narrow(pieces[0], *[col(pieces[m].astype(BF), m) for m in range(1, nc)])
        keyval_block, _ = chain_tok(keyval_mine)

        mix_three = narrow(*reduce_plane(mix[0][4:], True))
        mix_two = narrow(*reduce_plane(mix[0][:4], False), tok(mix_three, 1))
        mix_two = tok(mix_two, 2)
        late = [after(part, normed_grad) for part in mix[1]]
        mix_one = narrow(*reduce_plane(late[4:], True))
        mixture = total(
            *reduce_plane(late[:4], False), after(mix_two, normed_grad), tok(mix_one, 1)
        )
        layer_out = (after_attn + mixture).astype(BF)

        small = sum_small(
            jnp.concatenate(
                [
                    router_part.reshape(-1),
                    gain1_part,
                    gain2_part,
                    qgain_part.reshape(-1),
                    kgain_part.reshape(-1),
                ]
            )
        )
        edges = [0]
        for n in (D * experts, D, D, HD, HD):
            edges.append(edges[-1] + n)
        router_grad, norm1_grad, norm2_grad, query_gain_grad, key_gain_grad = (
            small[a:b] for a, b in zip(edges[:-1], edges[1:])
        )
        return (
            layer_out,
            input_grad,
            query_block,
            keyval_block,
            output_block,
            router_grad.reshape(D, experts),
            gate_up_grad[None],
            down_grad[None],
            norm1_grad,
            norm2_grad,
            query_gain_grad,
            key_gain_grad,
        )

    return per_device


def solution(mesh):
    by_all = P(ALL, None)
    by_expert = P(ALL, None, None)
    return jax.shard_map(
        build(dict(mesh.shape)),
        mesh=mesh,
        in_specs=(
            by_all,
            P(("tok", "row"), None),
            by_all,
            P(),
            P(),
            P(),
            P("row", "col"),
            P("row", "col"),
            P("col", "row"),
            P(),
            P(),
            by_expert,
            by_expert,
            by_all,
        ),
        out_specs=(
            by_all,
            by_all,
            P("row", "col"),
            P("row", "col"),
            P("col", "row"),
            P(),
            by_expert,
            by_expert,
            P(),
            P(),
            P(),
            P(),
        ),
        check_vma=False,
    )
```
